128 devices in a mesh: space: 64 (over x, y, z), level: 2 (over core).
Axes of the slice: x: 4, y: 4, z: 4, core: 2. Of those that a mesh axis runs over, the one named last changes fastest.
Arguments:
- multipole_fine: bfloat16 [512, 16, 16, 152], P('space'), may hold values from -6 to 6
- multipole_mid: bfloat16 [256, 8, 8, 152], P('space'), may hold values from -6 to 6
- multipole_coarse: bfloat16 [128, 4, 4, 152], P('space'), may hold values from -6 to 6
- multipole_top: bfloat16 [64, 2, 2, 152], P('space'), may hold values from -6 to 6
- translation_ops: bfloat16 [7, 7, 7, 152, 152], replicated, may hold values from -0.03125 to 0.03125
- upsample_ops: bfloat16 [2, 2, 2, 152, 152], replicated, may hold values from -0.5 to 0.5
Outputs:
- local_fine: float32 [512, 16, 16, 152], P('space', 'level')
The draws below stay inside these ranges and needn't reach their ends.
All inputs are finite; a program needn't handle non-finite values.
Results may differ from the reference program's by a relative error of at most 0.0003.
Values may be sent and summed in bfloat16 or wider, within the bound.
A program may use at most 448 MiB of HBM per device.

```python
import jax
import jax.numpy as jnp
from jax import lax

NCOEF = 152
NZ0 = 16
NX0 = 512
NY0 = 16
NX1 = 256
NY1 = 8
NZ1 = 8
NX2 = 128
NY2 = 4
NZ2 = 4
NX3 = 64
NY3 = 2
NZ3 = 2


def block_levels(key, dims, split, smallest, top_value):
    gain = 1.0
    for dim, blocks in split:
        heights = jax.random.uniform(jax.random.fold_in(jax.random.fold_in(key, 6), dim), (blocks,), jnp.float32, smallest / len(split), top_value / len(split))
        gain = gain * jnp.repeat(jnp.exp(heights), dims[dim] // blocks).reshape((-1,) + (1,) * (len(dims) - 1 - dim))
    return gain


def bell_draw(own_key, shape, width, bound, pieces=(), kind=jnp.bfloat16):
    entries = jax.random.normal(own_key, shape, jnp.float32) * width
    if len(pieces) > 0:
        entries = block_levels(own_key, shape, pieces, -0.22, 0.18) * entries
    return jnp.clip(entries, min=-bound, max=bound).astype(kind)


def setup_inputs(seed: int = 0) -> dict:
    key_of = jax.random.split(jax.random.key(seed), 7)
    return {
        "multipole_fine": bell_draw(key_of[0], (NX0, NY0, NZ0, NCOEF), 1.0, 6.0, ((0, 64),)),
        "multipole_mid": bell_draw(key_of[1], (NX1, NY1, NZ1, NCOEF), 1.0, 6.0, ((0, 64),)),
        "multipole_coarse": bell_draw(key_of[2], (NX2, NY2, NZ2, NCOEF), 1.0, 6.0, ((0, 64),)),
        "multipole_top": bell_draw(key_of[3], (NX3, NY3, NZ3, NCOEF), 1.0, 6.0, ((0, 64),)),
        "translation_ops": bell_draw(key_of[4], (7, 7, 7, NCOEF, NCOEF), (189 * NCOEF) ** -0.5, 0.03125),
        "upsample_ops": bell_draw(key_of[5], (2, 2, 2, NCOEF, NCOEF), NCOEF ** -0.5, 0.5),
    }


def near_blocks(number_type):
    position = jnp.arange(7)
    inside = (position >= 2) & (position <= 4)
    center = inside[:, None, None] & inside[None, :, None] & inside[None, None, :]
    return jnp.where(center, 0.0, 1.0).astype(number_type)[:, :, :, None, None]


def parity_kernels(masked_ops):
    channels = masked_ops.shape[-1]
    kernels = []
    for parity_x in range(2):
        for parity_y in range(2):
            for parity_z in range(2):
                window = masked_ops[1 - parity_x:7 - parity_x, 1 - parity_y:7 - parity_y, 1 - parity_z:7 - parity_z]
                window = window.reshape(3, 2, 3, 2, 3, 2, channels, channels)
                window = window.transpose(0, 2, 4, 1, 3, 5, 6, 7)
                kernels.append(window.reshape(-1, channels))
    return kernels


def grid_far(multipole, masked_ops):
    source = multipole.astype(jnp.float32)
    extended = jnp.pad(source, ((2, 2), (2, 2), (2, 2), (0, 0)))
    size_x, size_y, size_z, channels = extended.shape
    parity_grid = extended.reshape(size_x // 2, 2, size_y // 2, 2, size_z // 2, 2, channels)
    parity_grid = parity_grid.transpose(0, 2, 4, 1, 3, 5, 6)
    count_x = size_x // 2 - 2
    count_y = size_y // 2 - 2
    count_z = size_z // 2 - 2
    kernels = parity_kernels(masked_ops.astype(jnp.float32))
    kernel_all = jnp.stack(kernels, axis=1).reshape(-1, 8 * channels)

    def one_column(index_x):
        slab_rows = lax.dynamic_slice_in_dim(parity_grid, index_x, 3, 0)
        sections = []
        for step_x in range(3):
            for step_y in range(3):
                for step_z in range(3):
                    sections.append(slab_rows[step_x, step_y:step_y + count_y, step_z:step_z + count_z])
        stacked = jnp.stack(sections, axis=2).reshape(count_y * count_z, -1)
        return jnp.dot(stacked, kernel_all, preferred_element_type=jnp.float32, precision=lax.Precision.HIGHEST)

    columns = lax.map(one_column, jnp.arange(count_x, dtype=jnp.int32))
    joined = columns.reshape(count_x, count_y, count_z, 2, 2, 2, channels)
    joined = joined.transpose(0, 3, 1, 4, 2, 5, 6)
    return joined.reshape(2 * count_x, 2 * count_y, 2 * count_z, channels)


def upsample(parent, upsample_ops):
    children = jnp.einsum("xyzi,abcio->xaybzco", parent.astype(jnp.float32), upsample_ops.astype(jnp.float32), precision=lax.Precision.HIGHEST)
    size_x, size_y, size_z, channels = parent.shape
    return children.reshape(2 * size_x, 2 * size_y, 2 * size_z, channels)


def reference(multipole_fine, multipole_mid, multipole_coarse, multipole_top, translation_ops, upsample_ops):
    masked_ops = translation_ops * near_blocks(translation_ops.dtype)
    local_exp = grid_far(multipole_top, masked_ops)
    for multipole in (multipole_coarse, multipole_mid, multipole_fine):
        local_exp = grid_far(multipole, masked_ops) + upsample(local_exp, upsample_ops)
    return local_exp
```

```python
import jax
import jax.numpy as jnp
from jax import lax
from jax.experimental import pallas as pl
from jax.experimental.pallas import tpu as pltpu
from jax.sharding import PartitionSpec as P

BF = jnp.bfloat16
F32 = jnp.float32
MESH = pl.DeviceIdType.MESH
CH = 152
MAIN = 128
TAIL = CH - MAIN
ROWS = 160
NBLK = 10


def pad_tail(x):
    zeros = jnp.zeros(x.shape[:-1] + (MAIN - TAIL,), x.dtype)
    return jnp.concatenate([x, zeros], axis=x.ndim - 1)


def kernel(
    mf, mm, mc, mt, tr, up, out,
    tm, tt, um, ut, gb0, gb1, gb2, gb3,
    f0, t0, f1, t1, f2, t2, f3, t3,
    xb, xs, v, vu, acc, pm, pt, om, ot,
    tsem, gsem, send, recv,
):
    col = lax.axis_index("space")
    lev = lax.axis_index("level")
    n_col = lax.axis_size("space")
    par = col // 2
    base = 2 * par
    odd = lax.rem(col, 2)
    lo_ok = par > 0
    hi_ok = par < n_col // 2 - 1

    barrier = pltpu.get_barrier_semaphore()

    def greet(dev):
        pl.semaphore_signal(barrier, inc=1, device_id=(dev, lev), device_id_type=MESH)

    greet(base + 1 - odd)

    @pl.when(lo_ok)
    def _():
        greet(base - 2)
        greet(base - 1)

    @pl.when(hi_ok)
    def _():
        greet(base + 2)
        greet(base + 3)

    y0 = 6 * lev
    d0 = 2 * (1 - lev)
    y1 = 2 * lev
    loc0 = pltpu.make_async_copy(mf.at[:, pl.ds(y0, 10)], gb0.at[2:10, pl.ds(d0, 10)], gsem.at[0])
    loc1 = pltpu.make_async_copy(mm.at[:, pl.ds(y1, 6)], gb1.at[2:6, pl.ds(d0, 6)], gsem.at[1])
    loc2 = pltpu.make_async_copy(mc, gb2.at[2:4, pl.ds(d0, 4)], gsem.at[2])
    loc3 = pltpu.make_async_copy(mt, gb3.at[pl.ds(2 + odd, 1)], gsem.at[3])
    loc0.start()
    loc1.start()
    loc2.start()
    loc3.start()

    tcopies = {}

    def tcopy(kx, ysl, zsl, i):
        a = pltpu.make_async_copy(
            tr.at[kx, ysl, zsl, :, 0:MAIN], tm.at[kx, ysl, zsl, 0:CH, :], tsem.at[2 * i]
        )
        b = pltpu.make_async_copy(
            tr.at[kx, ysl, zsl, :, MAIN:CH], tt.at[kx, ysl, zsl, 0:CH, :], tsem.at[2 * i + 1]
        )
        a.start()
        b.start()
        tcopies.setdefault(kx, []).extend([a, b])

    idx = 0
    for kx in (2, 3, 4, 1, 0, 5, 6):
        if 2 <= kx <= 4:
            pieces = [
                (slice(0, 2), slice(0, 7)),
                (slice(5, 7), slice(0, 7)),
                (slice(2, 5), slice(0, 2)),
                (slice(2, 5), slice(5, 7)),
            ]
        else:
            pieces = [(slice(0, 7), slice(0, 7))]
        for ysl, zsl in pieces:
            tcopy(kx, ysl, zsl, idx)
            idx += 1
    cu_m = pltpu.make_async_copy(up.at[:, :, :, :, 0:MAIN], um.at[:, :, :, 0:CH, :], gsem.at[4])
    cu_t = pltpu.make_async_copy(up.at[:, :, :, :, MAIN:CH], ut.at[:, :, :, 0:CH, :], gsem.at[5])
    cu_m.start()
    cu_t.start()

    def halo(src, dst, i, dev, j=None):
        return pltpu.make_async_remote_copy(
            src_ref=src, dst_ref=dst, send_sem=send.at[i], recv_sem=recv.at[i if j is None else j],
            device_id=(dev, lev), device_id_type=MESH,
        )

    rights = [
        halo(mf.at[6:8, pl.ds(y0, 10)], gb0.at[0:2, pl.ds(d0, 10)], 0, col + 1),
        halo(mm.at[2:4, pl.ds(y1, 6)], gb1.at[0:2, pl.ds(d0, 6)], 1, col + 1),
        halo(mc, gb2.at[0:2, pl.ds(d0, 4)], 2, col + 1),
    ]
    lefts = [
        halo(mf.at[0:2, pl.ds(y0, 10)], gb0.at[10:12, pl.ds(d0, 10)], 3, col - 1),
        halo(mm.at[0:2, pl.ds(y1, 6)], gb1.at[6:8, pl.ds(d0, 6)], 4, col - 1),
        halo(mc, gb2.at[4:6, pl.ds(d0, 4)], 5, col - 1),
    ]
    top_partner = halo(mt, gb3.at[pl.ds(2 + odd, 1)], 6, base + 1 - odd)
    top_low = [
        halo(mt, gb3.at[pl.ds(4 + odd, 1)], 7 + i, base - 2 + i, 7 + odd) for i in range(2)
    ]
    top_high = [halo(mt, gb3.at[pl.ds(odd, 1)], 9 + i, base + 2 + i, 9 + odd) for i in range(2)]
    n_greet = 1 + jnp.where(lo_ok, 2, 0) + jnp.where(hi_ok, 2, 0)
    pl.semaphore_wait(barrier, n_greet)

    top_partner.start()

    @pl.when(lo_ok)
    def _():
        for c in top_low:
            c.start()

    @pl.when(hi_ok)
    def _():
        for c in top_high:
            c.start()

    @pl.when(col < n_col - 1)
    def _():
        for c in rights[::-1]:
            c.start()

    @pl.when(col > 0)
    def _():
        for c in lefts[::-1]:
            c.start()

    gb0[:, pl.ds(10 * lev, 2)] = jnp.zeros((12, 2, 16, CH), BF)
    gb1[:, pl.ds(6 * lev, 2)] = jnp.zeros((8, 2, 8, CH), BF)
    gb2[:, pl.ds(4 * lev, 2)] = jnp.zeros((6, 2, 4, CH), BF)

    @pl.when(col == 0)
    def _():
        gb0[0:2] = jnp.zeros((2, 12, 16, CH), BF)
        gb1[0:2] = jnp.zeros((2, 8, 8, CH), BF)
        gb2[0:2] = jnp.zeros((2, 6, 4, CH), BF)

    @pl.when(col == n_col - 1)
    def _():
        gb0[10:12] = jnp.zeros((2, 12, 16, CH), BF)
        gb1[6:8] = jnp.zeros((2, 8, 8, CH), BF)
        gb2[4:6] = jnp.zeros((2, 6, 4, CH), BF)

    @pl.when(par == 0)
    def _():
        gb3[0:2] = jnp.zeros((2, 2, 2, CH), BF)

    @pl.when(par == n_col // 2 - 1)
    def _():
        gb3[4:6] = jnp.zeros((2, 2, 2, CH), BF)

    def zero_edges(i, _):
        tm[i // 7, lax.rem(i, 7), :, CH:ROWS, :] = jnp.zeros((7, ROWS - CH, MAIN), BF)
        tt[i // 7, lax.rem(i, 7), :, CH:ROWS, :] = jnp.zeros((7, ROWS - CH, TAIL), BF)
        return 0

    lax.fori_loop(0, 49, zero_edges, 0)

    def zero_near(i, _):
        kx, ky, kz = 2 + i // 9, 2 + lax.rem(i // 3, 3), 2 + lax.rem(i, 3)
        tm[kx, ky, kz, 0:CH, :] = jnp.zeros((CH, MAIN), BF)
        tt[kx, ky, kz, 0:CH, :] = jnp.zeros((CH, TAIL), BF)
        return 0

    lax.fori_loop(0, 27, zero_near, 0)
    um[:, :, :, CH:ROWS, :] = jnp.zeros((2, 2, 2, ROWS - CH, MAIN), BF)
    ut[:, :, :, CH:ROWS, :] = jnp.zeros((2, 2, 2, ROWS - CH, TAIL), BF)
    f3[...] = jnp.zeros(f3.shape, F32)
    t3[...] = jnp.zeros(t3.shape, F32)

    def z_slots(tail, sy):
        even = lax.rem(lax.broadcasted_iota(jnp.int32, tail.shape, 0), 2) == 0
        a = pltpu.roll(tail, 64 * sy, 1) if sy else tail
        b = pltpu.roll(tail, 64 * sy + 32, 1)
        return jnp.where(even, a, b)

    z8 = jnp.zeros((8, MAIN), F32)

    def conv0(i, _):
        x, yp = i // 6, lax.rem(i, 6)
        tails = []
        for sy in range(2):
            y = 2 * yp + sy
            f0[x, y, 0:8, :] = z8
            f0[x, y, 24:32, :] = z8
            f0[x, y, 8:24, :] = gb0[x, y, :, 0:MAIN].astype(F32)
            tails.append(z_slots(pad_tail(gb0[x, y, :, MAIN:CH].astype(F32)), sy))
        t0[x, yp, 0:8, :] = z8
        t0[x, yp, 24:32, :] = z8
        t0[x, yp, 8:24, :] = tails[0] + tails[1]
        return 0

    def build0(i, _):
        xp, w = i // 9, lax.rem(i, 9)
        sty, stz = w // 3, lax.rem(w, 3)
        for sx in range(2):
            x = 2 * xp + sx
            for sy in range(2):
                for sz in range(2):
                    rows = [
                        f0[x, 2 * (py + sty) + sy, pl.ds(6 + 2 * stz + sz, 8, stride=2), :]
                        for py in range(4)
                    ]
                    s = 4 * sx + 2 * sy + sz
                    xb[w, s, xp] = jnp.concatenate(rows, axis=0).astype(BF)
            rows = [
                t0[x, py + sty, pl.ds(6 + 2 * stz, 8, stride=2), :]
                + t0[x, py + sty, pl.ds(7 + 2 * stz, 8, stride=2), :]
                for py in range(4)
            ]
            xb[w, 8 + sx, xp] = jnp.concatenate(rows, axis=0).astype(BF)
        return 0

    loc0.wait()
    lax.fori_loop(12, 60, conv0, 0)
    lax.fori_loop(9, 45, build0, 0)

    loc1.wait()
    loc2.wait()
    loc3.wait()

    @pl.when(col > 0)
    def _():
        for c in rights:
            c.wait_recv()

    @pl.when(col < n_col - 1)
    def _():
        for c in lefts:
            c.wait_recv()

    halo(mt, gb3.at[pl.ds(3 - odd, 1)], 6, base + 1 - odd).wait_recv()

    @pl.when(lo_ok)
    def _():
        for i in range(2):
            halo(mt, gb3.at[pl.ds(i, 1)], 9 + i, base - 2 + i).wait_recv()

    @pl.when(hi_ok)
    def _():
        for i in range(2):
            halo(mt, gb3.at[pl.ds(4 + i, 1)], 7 + i, base + 2 + i).wait_recv()

    lax.fori_loop(0, 12, conv0, 0)
    lax.fori_loop(60, 72, conv0, 0)
    lax.fori_loop(0, 9, build0, 0)
    lax.fori_loop(45, 54, build0, 0)

    def conv1(x, _):
        for sy in range(2):
            f1[x, sy, 0:8, :] = z8
            f1[x, sy, 40:48, :] = z8
        t1[x, 0:8, :] = z8
        t1[x, 40:48, :] = z8
        for yp in range(4):
            tails = []
            for sy in range(2):
                y = 2 * yp + sy
                f1[x, sy, 8 + 8 * yp : 16 + 8 * yp, :] = gb1[x, y, :, 0:MAIN].astype(F32)
                tails.append(z_slots(pad_tail(gb1[x, y, :, MAIN:CH].astype(F32)), sy))
            t1[x, 8 + 8 * yp : 16 + 8 * yp, :] = tails[0] + tails[1]
        return 0

    lax.fori_loop(0, 8, conv1, 0)

    def conv2(i, _):
        x, yp = i // 3, lax.rem(i, 3)
        tails = []
        for sy in range(2):
            y = 2 * yp + sy
            f2[x, y] = jnp.zeros((32, MAIN), F32)
            f2[x, y, 8:12, :] = gb2[x, y, :, 0:MAIN].astype(F32)
            tails.append(z_slots(pad_tail(gb2[x, y, :, MAIN:CH].astype(F32)), sy))
        t2[x, yp] = jnp.zeros((32, MAIN), F32)
        t2[x, yp, 8:12, :] = tails[0] + tails[1]
        return 0

    lax.fori_loop(0, 18, conv2, 0)

    def conv3(x, _):
        tails = []
        for y in range(2):
            f3[x, 2 + y, 8:10, :] = gb3[x, y, :, 0:MAIN].astype(F32)
            tails.append(z_slots(pad_tail(gb3[x, y, :, MAIN:CH].astype(F32)), y))
        t3[x, 1, 8:10, :] = tails[0] + tails[1]
        return 0

    lax.fori_loop(0, 6, conv3, 0)

    def build_small(i, _):
        stx, sty, stz = i // 9, lax.rem(i // 3, 3), lax.rem(i, 3)
        row = lax.broadcasted_iota(jnp.int32, (8, MAIN), 0)
        pz = lax.rem(row, 4) + stz - 1
        inside = (pz >= 0) & (pz < 4)

        def put(j, one, two, three):
            one = [jnp.where(inside, p, 0.0) for p in one]
            rest = jnp.where(row < 2, two, jnp.where(row == 2, three, 0.0))
            xs[i, j] = jnp.concatenate(one + [rest, z8], axis=0).astype(BF)

        for sx in range(2):
            for sy in range(2):
                for sz in range(2):
                    one = [
                        f1[2 * (px + stx) + sx, sy, pl.ds(6 + 8 * sty + 2 * stz + sz, 8, stride=2), :]
                        for px in range(2)
                    ]
                    two = f2[2 * stx + sx, 2 * sty + sy, pl.ds(6 + 2 * stz + sz, 8, stride=2), :]
                    three = f3[2 * stx + sx, 2 * sty + sy, pl.ds(2 + 2 * stz + sz, 8, stride=2), :]
                    put(4 * sx + 2 * sy + sz, one, two, three)
            one = [
                t1[2 * (px + stx) + sx, pl.ds(6 + 8 * sty + 2 * stz, 8, stride=2), :]
                + t1[2 * (px + stx) + sx, pl.ds(7 + 8 * sty + 2 * stz, 8, stride=2), :]
                for px in range(2)
            ]
            two = (
                t2[2 * stx + sx, sty, pl.ds(6 + 2 * stz, 8, stride=2), :]
                + t2[2 * stx + sx, sty, pl.ds(7 + 2 * stz, 8, stride=2), :]
            )
            three = (
                t3[2 * stx + sx, sty, pl.ds(2 + 2 * stz, 8, stride=2), :]
                + t3[2 * stx + sx, sty, pl.ds(3 + 2 * stz, 8, stride=2), :]
            )
            put(8 + sx, one, two, three)
        return 0

    lax.fori_loop(0, 27, build_small, 0)

    def tails_of(kx):
        def body(rz, _):
            last = None
            for ky in range(7):
                a = pad_tail(tt[kx, ky, rz + 1])
                b = pad_tail(tt[kx, ky, rz])
                pair = a + pltpu.roll(b, 32, 1)
                if last is not None:
                    v[(kx * 6 + ky - 1) * 6 + rz] = pair + last
                last = pltpu.roll(pair, 64, 1)
            return 0

        lax.fori_loop(0, 6, body, 0)

    def step(i, stx):
        sty, stz = i // 3, lax.rem(i, 3)
        t = stx * 9 + i
        lhs = jnp.concatenate(
            [
                jnp.concatenate(
                    [xb[i, j, stx : stx + 4].reshape(128, MAIN), xs[t, j]], axis=0
                )
                for j in range(NBLK)
            ],
            axis=1,
        )

        def accumulate(n, pick):
            mains = []
            tails = []
            for s in range(8):
                w = pick(s)
                mains.append(jnp.concatenate([x(0, MAIN) for x in w], axis=1))
                tails.append(jnp.concatenate([x(MAIN, ROWS) for x in w], axis=1))
            rhs = jnp.concatenate(mains + tails, axis=0)
            res = jnp.dot(lhs, rhs, preferred_element_type=F32)
            acc[2 * n] += res[:, 0:MAIN]
            acc[2 * n + 1] += res[:, MAIN:]

        def main_of(s, c):
            kx = 2 * stx + (s >> 2) - (c >> 2) + 1
            ky = 2 * sty + ((s >> 1) & 1) - ((c >> 1) & 1) + 1
            kz = 2 * stz + (s & 1) - (c & 1) + 1
            return lambda lo, hi: tm[kx, ky, kz, lo:hi, :]

        def tail_of(s, h):
            kx = 2 * stx + (s >> 2) - h + 1
            ry = 2 * sty + ((s >> 1) & 1)
            rz = 2 * stz + (s & 1)
            k = (kx * 6 + ry) * 6 + rz
            return lambda lo, hi: v[k, lo:hi, :]

        for n in range(4):
            accumulate(n, lambda s: [main_of(s, 2 * n), main_of(s, 2 * n + 1)])
        accumulate(4, lambda s: [tail_of(s, 0), tail_of(s, 1)])

    acc[...] = jnp.zeros(acc.shape, F32)
    for stx, slabs in ((1, (2, 3, 4)), (0, (1, 0)), (2, (5, 6))):
        for kx in slabs:
            for c in tcopies[kx]:
                c.wait()
            tails_of(kx)
        if stx == 1:

            def body(i, _):
                step(i + jnp.where(i >= 4, 1, 0), 1)
                return 0

            lax.fori_loop(0, 8, body, 0)
        else:

            def body(i, _, stx=stx):
                step(i, stx)
                return 0

            lax.fori_loop(0, 9, body, 0)

    cu_m.wait()
    cu_t.wait()
    for h in range(2):
        parts = [pad_tail(ut[h, q >> 1, q & 1]) for q in range(4)]
        total = parts[0]
        for q in range(1, 4):
            total = total + pltpu.roll(parts[q], 32 * q, 1)
        vu[h] = total

    def upsampled(main, tail):
        rows = main.shape[0]
        hi_m = main.astype(BF)
        lo_m = (main - hi_m.astype(F32)).astype(BF)
        hi_t = tail.astype(BF).astype(F32)
        both = (hi_t + pltpu.roll(tail - hi_t, 32, 1)).astype(BF)
        lhs = jnp.concatenate([hi_m, lo_m, both], axis=1)

        def rhs_of(x):
            return jnp.concatenate(
                [x(0, MAIN), x(0, MAIN), x(MAIN, ROWS), x(MAIN, ROWS), jnp.zeros((64, MAIN), BF)],
                axis=0,
            )

        cols = []
        for n in range(5):
            if n < 4:
                pair = [
                    rhs_of(lambda lo, hi, c=c: um[c >> 2, (c >> 1) & 1, c & 1, lo:hi, :])
                    for c in (2 * n, 2 * n + 1)
                ]
            else:
                pair = [rhs_of(lambda lo, hi, h=h: vu[h, lo:hi, :]) for h in range(2)]
            res = jnp.dot(lhs, jnp.concatenate(pair, axis=1), preferred_element_type=F32)
            cols += [res[:, 0:MAIN], res[:, MAIN:]]
        return cols

    def tail_lanes(x, c):
        q = c & 3
        y = pltpu.roll(x, MAIN - 32 * q, 1) if q else x
        lane = lax.broadcasted_iota(jnp.int32, x.shape, 1)
        return jnp.where(lane < TAIL, y, 0.0)

    pm[...] = jnp.zeros(pm.shape, F32)
    pt[...] = jnp.zeros(pt.shape, F32)
    rest = [acc[j, 144:152, :] for j in range(NBLK)]
    for cz in range(2):
        mains = [rest[4 * a + 2 * b + cz] for a in range(2) for b in range(2)]
        tails = [
            tail_lanes(rest[8 + a], 4 * a + 2 * b + cz) for a in range(2) for b in range(2)
        ]

        def choose(four):
            low = jnp.where(lev == 0, four[0], four[1])
            high = jnp.where(lev == 0, four[2], four[3])
            return jnp.where(odd == 0, low, high)

        pm[cz : cz + 1, :] = choose(mains)[2:3]
        pt[cz : cz + 1, :] = choose(tails)[2:3]
    add = upsampled(pm[0:16, :], pt[0:16, :])
    local2 = [rest[j] + add[j][0:8] for j in range(NBLK)]
    for c in range(8):
        cx, cy, cz = c >> 2, (c >> 1) & 1, c & 1
        tail = tail_lanes(local2[8 + cx], c)
        for p in range(2):
            r = 8 * cx + 4 * cy + 2 * p + cz
            pm[16 + r : 17 + r, :] = local2[c][p : p + 1]
            pt[16 + r : 17 + r, :] = tail[p : p + 1]
    add = upsampled(pm[16:32, :], pt[16:32, :])
    local1 = [acc[j, 128:144, :] + add[j] for j in range(NBLK)]
    for c in range(8):
        cx, cy, cz = c >> 2, (c >> 1) & 1, c & 1
        tail = tail_lanes(local1[8 + cx], c)
        for px in range(2):
            for py in range(2):
                r = 32 + 32 * (2 * px + cx) + 8 * (2 * py + cy) + cz
                q = 8 * px + 4 * py
                pm[pl.ds(r, 4, stride=2), :] = local1[c][q : q + 4]
                pt[pl.ds(r, 4, stride=2), :] = tail[q : q + 4]
    add = upsampled(pm[32:160, :], pt[32:160, :])
    for c in range(8):
        cx, cy, cz = c >> 2, (c >> 1) & 1, c & 1
        main = acc[c, 0:128, :] + add[c]
        tail = tail_lanes(acc[8 + cx, 0:128, :] + add[8 + cx], c)
        for px in range(4):
            for py in range(4):
                q = 32 * px + 8 * py
                x, y = 2 * px + cx, 2 * py + cy
                om[8 * x + y, pl.ds(cz, 8, stride=2), :] = main[q : q + 8]
                ot[8 * x + y, pl.ds(cz, 8, stride=2), :] = tail[q : q + 8]

    def emit(x, _):
        for y in range(8):
            out[x, y, :, 0:MAIN] = om[8 * x + y]
            out[x, y, :, MAIN:CH] = ot[8 * x + y][:, 0:TAIL]
        return 0

    lax.fori_loop(0, 8, emit, 0)

    top_partner.wait_send()

    @pl.when(lo_ok)
    def _():
        for c in top_low:
            c.wait_send()

    @pl.when(hi_ok)
    def _():
        for c in top_high:
            c.wait_send()

    @pl.when(col < n_col - 1)
    def _():
        for c in rights:
            c.wait_send()

    @pl.when(col > 0)
    def _():
        for c in lefts:
            c.wait_send()


def shards(
    multipole_fine, multipole_mid, multipole_coarse, multipole_top, translation_ops, upsample_ops
):
    vmem = pltpu.VMEM
    return pl.pallas_call(
        kernel,
        out_shape=jax.ShapeDtypeStruct((8, 8, 16, CH), F32),
        in_specs=[pl.BlockSpec(memory_space=pl.ANY)] * 6,
        out_specs=pl.BlockSpec(memory_space=pltpu.VMEM),
        scratch_shapes=[
            vmem((7, 7, 7, ROWS, MAIN), BF),
            vmem((7, 7, 7, ROWS, TAIL), BF),
            vmem((2, 2, 2, ROWS, MAIN), BF),
            vmem((2, 2, 2, ROWS, TAIL), BF),
            vmem((12, 12, 16, CH), BF),
            vmem((8, 8, 8, CH), BF),
            vmem((6, 6, 4, CH), BF),
            vmem((6, 2, 2, CH), BF),
            vmem((12, 12, 32, MAIN), F32),
            vmem((12, 6, 32, MAIN), F32),
            vmem((8, 2, 48, MAIN), F32),
            vmem((8, 48, MAIN), F32),
            vmem((6, 6, 32, MAIN), F32),
            vmem((6, 3, 32, MAIN), F32),
            vmem((6, 6, 32, MAIN), F32),
            vmem((6, 3, 32, MAIN), F32),
            vmem((9, NBLK, 6, 32, MAIN), BF),
            vmem((27, NBLK, 32, MAIN), BF),
            vmem((7 * 36, ROWS, MAIN), BF),
            vmem((2, ROWS, MAIN), BF),
            vmem((NBLK, 160, MAIN), F32),
            vmem((160, MAIN), F32),
            vmem((160, MAIN), F32),
            vmem((64, 16, MAIN), F32),
            vmem((64, 16, MAIN), F32),
            pltpu.SemaphoreType.DMA((32,)),
            pltpu.SemaphoreType.DMA((6,)),
            pltpu.SemaphoreType.DMA((11,)),
            pltpu.SemaphoreType.DMA((11,)),
        ],
        compiler_params=pltpu.CompilerParams(
            collective_id=0, has_side_effects=True, vmem_limit_bytes=66_000_000
        ),
        name="downward",
    )(multipole_fine, multipole_mid, multipole_coarse, multipole_top, translation_ops, upsample_ops)


def solution(mesh):
    placed = (
        P("space", None, None, None),
        P("space", None, None, None),
        P("space", None, None, None),
        P("space", None, None, None),
        P(),
        P(),
    )
    return jax.shard_map(
        shards,
        mesh=mesh,
        in_specs=placed,
        out_specs=P("space", "level", None, None),
        check_vma=False,
    )
```

```python
import jax
import jax.numpy as jnp
from jax import lax
from jax.experimental import pallas as pl
from jax.experimental.pallas import tpu as pltpu
from jax.sharding import PartitionSpec as P

BF = jnp.bfloat16
F32 = jnp.float32
MESH = pl.DeviceIdType.MESH
CH = 152
MAIN = 128
TAIL = CH - MAIN
ROWS = 160
NBLK = 10


def pad_tail(x):
    zeros = jnp.zeros(x.shape[:-1] + (MAIN - TAIL,), x.dtype)
    return jnp.concatenate([x, zeros], axis=x.ndim - 1)


def kernel(
    mf, mm, mc, mt, tr, up, out,
    tm, tt, um, ut, gb0, gb1, gb2, gb3,
    f0, t0, f1, t1, f2, t2, f3, t3,
    xm, xe, xsm, xse, v, vu, acc, pm, pt, om, ot,
    tsem, gsem, send, recv,
):
    col = lax.axis_index("space")
    lev = lax.axis_index("level")
    n_col = lax.axis_size("space")
    par = col // 2
    base = 2 * par
    odd = lax.rem(col, 2)
    lo_ok = par > 0
    hi_ok = par < n_col // 2 - 1

    barrier = pltpu.get_barrier_semaphore()

    def greet(dev):
        pl.semaphore_signal(barrier, inc=1, device_id=(dev, lev), device_id_type=MESH)

    greet(base + 1 - odd)

    @pl.when(lo_ok)
    def _():
        greet(base - 2)
        greet(base - 1)

    @pl.when(hi_ok)
    def _():
        greet(base + 2)
        greet(base + 3)

    y0 = 6 * lev
    d0 = 2 * (1 - lev)
    y1 = 2 * lev
    loc0 = pltpu.make_async_copy(mf.at[:, pl.ds(y0, 10)], gb0.at[2:10, pl.ds(d0, 10)], gsem.at[0])
    loc1 = pltpu.make_async_copy(mm.at[:, pl.ds(y1, 6)], gb1.at[2:6, pl.ds(d0, 6)], gsem.at[1])
    loc2 = pltpu.make_async_copy(mc, gb2.at[2:4, pl.ds(d0, 4)], gsem.at[2])
    loc3 = pltpu.make_async_copy(mt, gb3.at[pl.ds(2 + odd, 1)], gsem.at[3])
    loc0.start()
    loc1.start()
    loc2.start()
    loc3.start()

    tcopies = {}

    def tcopy(kx, ysl, zsl, i):
        a = pltpu.make_async_copy(
            tr.at[kx, ysl, zsl, :, 0:MAIN], tm.at[kx, ysl, zsl, 0:CH, :], tsem.at[2 * i]
        )
        b = pltpu.make_async_copy(
            tr.at[kx, ysl, zsl, :, MAIN:CH], tt.at[kx, ysl, zsl, 0:CH, :], tsem.at[2 * i + 1]
        )
        a.start()
        b.start()
        tcopies.setdefault(kx, []).extend([a, b])

    idx = 0
    for kx in (2, 3, 4, 1, 0, 5, 6):
        if 2 <= kx <= 4:
            pieces = [
                (slice(0, 2), slice(0, 7)),
                (slice(5, 7), slice(0, 7)),
                (slice(2, 5), slice(0, 2)),
                (slice(2, 5), slice(5, 7)),
            ]
        else:
            pieces = [(slice(0, 7), slice(0, 7))]
        for ysl, zsl in pieces:
            tcopy(kx, ysl, zsl, idx)
            idx += 1
    cu_m = pltpu.make_async_copy(up.at[:, :, :, :, 0:MAIN], um.at[:, :, :, 0:CH, :], gsem.at[4])
    cu_t = pltpu.make_async_copy(up.at[:, :, :, :, MAIN:CH], ut.at[:, :, :, 0:CH, :], gsem.at[5])
    cu_m.start()
    cu_t.start()

    def halo(src, dst, i, dev, j=None):
        return pltpu.make_async_remote_copy(
            src_ref=src, dst_ref=dst, send_sem=send.at[i], recv_sem=recv.at[i if j is None else j],
            device_id=(dev, lev), device_id_type=MESH,
        )

    rights = [
        halo(mf.at[6:8, pl.ds(y0, 10)], gb0.at[0:2, pl.ds(d0, 10)], 0, col + 1),
        halo(mm.at[2:4, pl.ds(y1, 6)], gb1.at[0:2, pl.ds(d0, 6)], 1, col + 1),
        halo(mc, gb2.at[0:2, pl.ds(d0, 4)], 2, col + 1),
    ]
    lefts = [
        halo(mf.at[0:2, pl.ds(y0, 10)], gb0.at[10:12, pl.ds(d0, 10)], 3, col - 1),
        halo(mm.at[0:2, pl.ds(y1, 6)], gb1.at[6:8, pl.ds(d0, 6)], 4, col - 1),
        halo(mc, gb2.at[4:6, pl.ds(d0, 4)], 5, col - 1),
    ]
    top_partner = halo(mt, gb3.at[pl.ds(2 + odd, 1)], 6, base + 1 - odd)
    top_low = [
        halo(mt, gb3.at[pl.ds(4 + odd, 1)], 7 + i, base - 2 + i, 7 + odd) for i in range(2)
    ]
    top_high = [halo(mt, gb3.at[pl.ds(odd, 1)], 9 + i, base + 2 + i, 9 + odd) for i in range(2)]
    n_greet = 1 + jnp.where(lo_ok, 2, 0) + jnp.where(hi_ok, 2, 0)
    z8 = jnp.zeros((8, MAIN), F32)
    gb0[:, pl.ds(10 * lev, 2)] = jnp.zeros((12, 2, 16, CH), BF)
    gb1[:, pl.ds(6 * lev, 2)] = jnp.zeros((8, 2, 8, CH), BF)
    gb2[:, pl.ds(4 * lev, 2)] = jnp.zeros((6, 2, 4, CH), BF)

    @pl.when(col == 0)
    def _():
        gb0[0:2] = jnp.zeros((2, 12, 16, CH), BF)
        gb1[0:2] = jnp.zeros((2, 8, 8, CH), BF)
        gb2[0:2] = jnp.zeros((2, 6, 4, CH), BF)

    @pl.when(col == n_col - 1)
    def _():
        gb0[10:12] = jnp.zeros((2, 12, 16, CH), BF)
        gb1[6:8] = jnp.zeros((2, 8, 8, CH), BF)
        gb2[4:6] = jnp.zeros((2, 6, 4, CH), BF)

    @pl.when(par == 0)
    def _():
        gb3[0:2] = jnp.zeros((2, 2, 2, CH), BF)

    @pl.when(par == n_col // 2 - 1)
    def _():
        gb3[4:6] = jnp.zeros((2, 2, 2, CH), BF)

    def zero_edges(kx, _):
        for ky in range(7):
            tm[kx, ky, :, CH:ROWS, :] = jnp.zeros((7, ROWS - CH, MAIN), BF)
            tt[kx, ky, :, CH:ROWS, :] = jnp.zeros((7, ROWS - CH, TAIL), BF)
        return 0

    lax.fori_loop(0, 7, zero_edges, 0)

    def zero_near(i, _):
        for kz in range(2, 5):
            tm[2 + i // 3, 2 + lax.rem(i, 3), kz, 0:CH, :] = jnp.zeros((CH, MAIN), BF)
            tt[2 + i // 3, 2 + lax.rem(i, 3), kz, 0:CH, :] = jnp.zeros((CH, TAIL), BF)
        return 0

    lax.fori_loop(0, 9, zero_near, 0)
    um[:, :, :, CH:ROWS, :] = jnp.zeros((2, 2, 2, ROWS - CH, MAIN), BF)
    ut[:, :, :, CH:ROWS, :] = jnp.zeros((2, 2, 2, ROWS - CH, TAIL), BF)

    def zero_pads(x, _):
        for y in range(12):
            f0[x, y, 0:8, :] = z8
            f0[x, y, 24:32, :] = z8
        for yp in range(6):
            t0[x, yp, 0:8, :] = z8
            t0[x, yp, 24:32, :] = z8
        return 0

    lax.fori_loop(0, 12, zero_pads, 0)

    def zero_coarse(x, _):
        f2[x] = jnp.zeros((6, 32, MAIN), F32)
        f3[x] = jnp.zeros((6, 32, MAIN), F32)
        t2[x] = jnp.zeros((3, 32, MAIN), F32)
        t3[x] = jnp.zeros((3, 32, MAIN), F32)
        return 0

    lax.fori_loop(0, 6, zero_coarse, 0)

    def zero_mid(x, _):
        for sy in range(2):
            f1[x, sy, 0:8, :] = z8
            f1[x, sy, 40:48, :] = z8
        t1[x, 0:8, :] = z8
        t1[x, 40:48, :] = z8
        return 0

    lax.fori_loop(0, 8, zero_mid, 0)

    def z_slots(tail, sy):
        even = lax.rem(lax.broadcasted_iota(jnp.int32, tail.shape, 0), 2) == 0
        a = pltpu.roll(tail, 64 * sy, 1) if sy else tail
        b = pltpu.roll(tail, 64 * sy + 32, 1)
        return jnp.where(even, a, b)

    def conv0(x):
        for yp in range(6):
            tails = []
            for sy in range(2):
                y = 2 * yp + sy
                f0[x, y, 8:24, :] = gb0[x, y, :, 0:MAIN].astype(F32)
                tails.append(z_slots(pad_tail(gb0[x, y, :, MAIN:CH].astype(F32)), sy))
            t0[x, yp, 8:24, :] = tails[0] + tails[1]

    def build0(xp, w, store):
        sty, stz = (w // 3, w % 3) if isinstance(w, int) else (w // 3, lax.rem(w, 3))
        for sx in range(2):
            x = 2 * xp + sx
            for sy in range(2):
                for sz in range(2):
                    rows = [
                        f0[x, 2 * (py + sty) + sy, pl.ds(6 + 2 * stz + sz, 8, stride=2), :]
                        for py in range(4)
                    ]
                    store(w, 4 * sx + 2 * sy + sz, jnp.concatenate(rows, axis=0).astype(BF))
            rows = [
                t0[x, py + sty, pl.ds(6 + 2 * stz, 8, stride=2), :]
                + t0[x, py + sty, pl.ds(7 + 2 * stz, 8, stride=2), :]
                for py in range(4)
            ]
            store(w, 8 + sx, jnp.concatenate(rows, axis=0).astype(BF))

    with jax.named_scope("conv_own"):
        loc0.wait()

        def own_conv(x, _):
            conv0(x)
            return 0

        lax.fori_loop(2, 10, own_conv, 0)

    with jax.named_scope("greet"):
        pl.semaphore_wait(barrier, n_greet)

        top_partner.start()

        @pl.when(lo_ok)
        def _():
            for c in top_low:
                c.start()

        @pl.when(hi_ok)
        def _():
            for c in top_high:
                c.start()

        @pl.when(col < n_col - 1)
        def _():
            for c in rights[::-1]:
                c.start()

        @pl.when(col > 0)
        def _():
            for c in lefts[::-1]:
                c.start()

    with jax.named_scope("build_own"):

        def own_build(w, _):
            for xp in range(1, 5):

                def store(w, j, val, xp=xp):
                    xm[w, j, xp - 1] = val

                build0(xp, w, store)
            return 0

        lax.fori_loop(0, 9, own_build, 0)

    with jax.named_scope("wait_small"):
        loc1.wait()
        loc2.wait()
        loc3.wait()

        @pl.when(col > 0)
        def _():
            for c in rights[1:]:
                c.wait_recv()

        @pl.when(col < n_col - 1)
        def _():
            for c in lefts[1:]:
                c.wait_recv()

        halo(mt, gb3.at[pl.ds(3 - odd, 1)], 6, base + 1 - odd).wait_recv()

        @pl.when(lo_ok)
        def _():
            for i in range(2):
                halo(mt, gb3.at[pl.ds(i, 1)], 9 + i, base - 2 + i).wait_recv()

        @pl.when(hi_ok)
        def _():
            for i in range(2):
                halo(mt, gb3.at[pl.ds(4 + i, 1)], 7 + i, base + 2 + i).wait_recv()

    def conv1(i, _):
        for k in range(2):
            x = 2 * i + k
            for yp in range(4):
                tails = []
                for sy in range(2):
                    y = 2 * yp + sy
                    f1[x, sy, 8 + 8 * yp : 16 + 8 * yp, :] = gb1[x, y, :, 0:MAIN].astype(F32)
                    tails.append(z_slots(pad_tail(gb1[x, y, :, MAIN:CH].astype(F32)), sy))
                t1[x, 8 + 8 * yp : 16 + 8 * yp, :] = tails[0] + tails[1]
        return 0

    def conv23():
        for x in range(6):
            for yp in range(3):
                tails = []
                for sy in range(2):
                    y = 2 * yp + sy
                    f2[x, y, 8:12, :] = gb2[x, y, :, 0:MAIN].astype(F32)
                    tails.append(z_slots(pad_tail(gb2[x, y, :, MAIN:CH].astype(F32)), sy))
                t2[x, yp, 8:12, :] = tails[0] + tails[1]
            tails = []
            for y in range(2):
                f3[x, 2 + y, 8:10, :] = gb3[x, y, :, 0:MAIN].astype(F32)
                tails.append(z_slots(pad_tail(gb3[x, y, :, MAIN:CH].astype(F32)), y))
            t3[x, 1, 8:10, :] = tails[0] + tails[1]

    with jax.named_scope("conv_small"):
        lax.fori_loop(0, 4, conv1, 0)
        conv23()

    def build_small(stx, sty, stz, store):
        row = lax.broadcasted_iota(jnp.int32, (8, MAIN), 0)
        pz = lax.rem(row, 4) + stz - 1
        inside = (pz >= 0) & (pz < 4)

        def put(j, one, two, three):
            one = [jnp.where(inside, p, 0.0) for p in one]
            rest = jnp.where(row < 2, two, jnp.where(row == 2, three, 0.0))
            store(3 * sty + stz, j, jnp.concatenate(one + [rest, z8], axis=0).astype(BF))

        for sx in range(2):
            for sy in range(2):
                for sz in range(2):
                    one = [
                        f1[2 * (px + stx) + sx, sy, pl.ds(6 + 8 * sty + 2 * stz + sz, 8, stride=2), :]
                        for px in range(2)
                    ]
                    two = f2[2 * stx + sx, 2 * sty + sy, pl.ds(6 + 2 * stz + sz, 8, stride=2), :]
                    three = f3[2 * stx + sx, 2 * sty + sy, pl.ds(2 + 2 * stz + sz, 8, stride=2), :]
                    put(4 * sx + 2 * sy + sz, one, two, three)
            one = [
                t1[2 * (px + stx) + sx, pl.ds(6 + 8 * sty + 2 * stz, 8, stride=2), :]
                + t1[2 * (px + stx) + sx, pl.ds(7 + 8 * sty + 2 * stz, 8, stride=2), :]
                for px in range(2)
            ]
            two = (
                t2[2 * stx + sx, sty, pl.ds(6 + 2 * stz, 8, stride=2), :]
                + t2[2 * stx + sx, sty, pl.ds(7 + 2 * stz, 8, stride=2), :]
            )
            three = (
                t3[2 * stx + sx, sty, pl.ds(2 + 2 * stz, 8, stride=2), :]
                + t3[2 * stx + sx, sty, pl.ds(3 + 2 * stz, 8, stride=2), :]
            )
            put(8 + sx, one, two, three)

    with jax.named_scope("build_small"):

        def small_mid(sty, _):
            def store(w, j, val):
                xsm[w, j] = val

            for stz in range(3):
                build_small(1, sty, stz, store)
            return 0

        lax.fori_loop(0, 3, small_mid, 0)

    def tail_unit(kx, rz):
        last = None
        for ky in range(7):
            a = pad_tail(tt[kx, ky, rz + 1])
            b = pad_tail(tt[kx, ky, rz])
            pair = a + pltpu.roll(b, 32, 1)
            if last is not None:
                v[(kx * 6 + ky - 1) * 6 + rz] = pair + last
            last = pltpu.roll(pair, 64, 1)

    def lhs_of(stx, sty, stzs):
        parts = []
        for stz in stzs:
            w = 3 * sty + stz
            for j in range(NBLK):
                if stx == 1:
                    rows = [xm[w, j].reshape(128, MAIN), xsm[w, j]]
                elif stx == 0:
                    rows = [xe[0, w, j], xm[w, j, 0:3].reshape(96, MAIN), xse[0, w, j]]
                else:
                    rows = [xm[w, j, 1:4].reshape(96, MAIN), xe[1, w, j], xse[1, w, j]]
                parts.append(jnp.concatenate(rows, axis=0))
        return jnp.concatenate(parts, axis=1)

    def dot_n(n, stx, sty, stzs):
        blocks = []
        for stz in stzs:
            mains = []
            tails = []
            for s in range(8):
                sx, sy, sz = s >> 2, (s >> 1) & 1, s & 1
                pair = []
                for h in range(2):
                    if n < 4:
                        c = 2 * n + h
                        kx = 2 * stx + sx - (c >> 2) + 1
                        ky = 2 * sty + sy - ((c >> 1) & 1) + 1
                        kz = 2 * stz + sz - (c & 1) + 1
                        pair.append((tm[kx, ky, kz, 0:MAIN, :], tm[kx, ky, kz, MAIN:ROWS, :]))
                    else:
                        k = ((2 * stx + sx - h + 1) * 6 + 2 * sty + sy) * 6 + 2 * stz + sz
                        pair.append((v[k, 0:MAIN, :], v[k, MAIN:ROWS, :]))
                mains.append(jnp.concatenate([p[0] for p in pair], axis=1))
                tails.append(jnp.concatenate([p[1] for p in pair], axis=1))
            blocks += mains + tails
        rhs = jnp.concatenate(blocks, axis=0)
        res = jnp.dot(lhs_of(stx, sty, stzs), rhs, preferred_element_type=F32)
        acc[2 * n] += res[:, 0:MAIN]
        acc[2 * n + 1] += res[:, MAIN:]

    def block(stx, sty, stzs, fill):
        for n in range(4):
            dot_n(n, stx, sty, stzs)
            for k in range(n * len(fill) // 4, (n + 1) * len(fill) // 4):
                fill[k]()

    def wait_t(*slabs):
        for kx in slabs:
            for c in tcopies[kx]:
                c.wait()

    acc[...] = jnp.zeros(acc.shape, F32)
    with jax.named_scope("wait_t"):
        wait_t(2, 3, 4)
    with jax.named_scope("mxu1"):

        def body(i, _):
            units = [
                lambda kx=kx, q=q: tail_unit(kx, 3 * i + q) for q in range(3) for kx in (2, 3, 4)
            ]
            block(1, 2 * i, (0, 1, 2), units)
            return 0

        lax.fori_loop(0, 2, body, 0)

    with jax.named_scope("wait_halo"):

        @pl.when(col > 0)
        def _():
            rights[0].wait_recv()

        @pl.when(col < n_col - 1)
        def _():
            lefts[0].wait_recv()

    with jax.named_scope("mxu1c"):
        fill = [lambda x=x: conv0(x) for x in (0, 1, 10, 11)]
        for w in range(9):
            for side in range(2):

                def edge(w=w, side=side):
                    def store(w, j, val):
                        xe[side, w, j] = val

                    build0(5 * side, w, store)

                def small(w=w, side=side):
                    def store(w, j, val):
                        xse[side, w, j] = val

                    build_small(2 * side, w // 3, w % 3, store)

                fill += [edge, small]
        block(1, 1, (0, 2), fill)
    for stx, slabs in ((0, (1, 0)), (2, (5, 6))):
        with jax.named_scope("wait_t"):
            wait_t(*slabs)
        with jax.named_scope("mxu02"):

            def body(sty, _, stx=stx, slabs=slabs):
                units = [
                    lambda kx=kx, q=q: tail_unit(kx, 2 * sty + q) for q in range(2) for kx in slabs
                ]
                block(stx, sty, (0, 1, 2), units)
                return 0

            lax.fori_loop(0, 3, body, 0)
    with jax.named_scope("mxu_tail"):
        for stx in range(3):

            def body(sty, _, stx=stx):
                dot_n(4, stx, sty, (0, 1, 2))
                return 0

            lax.fori_loop(0, 3, body, 0)

    cu_m.wait()
    cu_t.wait()
    for h in range(2):
        parts = [pad_tail(ut[h, q >> 1, q & 1]) for q in range(4)]
        total = parts[0]
        for q in range(1, 4):
            total = total + pltpu.roll(parts[q], 32 * q, 1)
        vu[h] = total

    def upsampled(main, tail):
        rows = main.shape[0]
        hi_m = main.astype(BF)
        lo_m = (main - hi_m.astype(F32)).astype(BF)
        hi_t = tail.astype(BF).astype(F32)
        both = (hi_t + pltpu.roll(tail - hi_t, 32, 1)).astype(BF)
        lhs = jnp.concatenate([hi_m, lo_m, both], axis=1)

        def rhs_of(x):
            return jnp.concatenate(
                [x(0, MAIN), x(0, MAIN), x(MAIN, ROWS), x(MAIN, ROWS), jnp.zeros((64, MAIN), BF)],
                axis=0,
            )

        cols = []
        for n in range(5):
            if n < 4:
                pair = [
                    rhs_of(lambda lo, hi, c=c: um[c >> 2, (c >> 1) & 1, c & 1, lo:hi, :])
                    for c in (2 * n, 2 * n + 1)
                ]
            else:
                pair = [rhs_of(lambda lo, hi, h=h: vu[h, lo:hi, :]) for h in range(2)]
            res = jnp.dot(lhs, jnp.concatenate(pair, axis=1), preferred_element_type=F32)
            cols += [res[:, 0:MAIN], res[:, MAIN:]]
        return cols

    def tail_lanes(x, c):
        q = c & 3
        y = pltpu.roll(x, MAIN - 32 * q, 1) if q else x
        lane = lax.broadcasted_iota(jnp.int32, x.shape, 1)
        return jnp.where(lane < TAIL, y, 0.0)

    pm[...] = jnp.zeros(pm.shape, F32)
    pt[...] = jnp.zeros(pt.shape, F32)
    rest = [acc[j, 144:152, :] for j in range(NBLK)]
    for cz in range(2):
        mains = [rest[4 * a + 2 * b + cz] for a in range(2) for b in range(2)]
        tails = [
            tail_lanes(rest[8 + a], 4 * a + 2 * b + cz) for a in range(2) for b in range(2)
        ]

        def choose(four):
            low = jnp.where(lev == 0, four[0], four[1])
            high = jnp.where(lev == 0, four[2], four[3])
            return jnp.where(odd == 0, low, high)

        pm[cz : cz + 1, :] = choose(mains)[2:3]
        pt[cz : cz + 1, :] = choose(tails)[2:3]
    add = upsampled(pm[0:16, :], pt[0:16, :])
    local2 = [rest[j] + add[j][0:8] for j in range(NBLK)]
    for c in range(8):
        cx, cy, cz = c >> 2, (c >> 1) & 1, c & 1
        tail = tail_lanes(local2[8 + cx], c)
        for p in range(2):
            r = 8 * cx + 4 * cy + 2 * p + cz
            pm[16 + r : 17 + r, :] = local2[c][p : p + 1]
            pt[16 + r : 17 + r, :] = tail[p : p + 1]
    add = upsampled(pm[16:32, :], pt[16:32, :])
    local1 = [acc[j, 128:144, :] + add[j] for j in range(NBLK)]
    for c in range(8):
        cx, cy, cz = c >> 2, (c >> 1) & 1, c & 1
        tail = tail_lanes(local1[8 + cx], c)
        for px in range(2):
            for py in range(2):
                r = 32 + 32 * (2 * px + cx) + 8 * (2 * py + cy) + cz
                q = 8 * px + 4 * py
                pm[pl.ds(r, 4, stride=2), :] = local1[c][q : q + 4]
                pt[pl.ds(r, 4, stride=2), :] = tail[q : q + 4]
    add = upsampled(pm[32:160, :], pt[32:160, :])
    for c in range(8):
        cx, cy, cz = c >> 2, (c >> 1) & 1, c & 1
        main = acc[c, 0:128, :] + add[c]
        tail = tail_lanes(acc[8 + cx, 0:128, :] + add[8 + cx], c)
        for px in range(4):
            for py in range(4):
                q = 32 * px + 8 * py
                x, y = 2 * px + cx, 2 * py + cy
                om[8 * x + y, pl.ds(cz, 8, stride=2), :] = main[q : q + 8]
                ot[8 * x + y, pl.ds(cz, 8, stride=2), :] = tail[q : q + 8]

    def emit(x, _):
        for y in range(8):
            out[x, y, :, 0:MAIN] = om[8 * x + y]
            out[x, y, :, MAIN:CH] = ot[8 * x + y][:, 0:TAIL]
        return 0

    lax.fori_loop(0, 8, emit, 0)

    top_partner.wait_send()

    @pl.when(lo_ok)
    def _():
        for c in top_low:
            c.wait_send()

    @pl.when(hi_ok)
    def _():
        for c in top_high:
            c.wait_send()

    @pl.when(col < n_col - 1)
    def _():
        for c in rights:
            c.wait_send()

    @pl.when(col > 0)
    def _():
        for c in lefts:
            c.wait_send()


def shards(
    multipole_fine, multipole_mid, multipole_coarse, multipole_top, translation_ops, upsample_ops
):
    vmem = pltpu.VMEM
    return pl.pallas_call(
        kernel,
        out_shape=jax.ShapeDtypeStruct((8, 8, 16, CH), F32),
        in_specs=[pl.BlockSpec(memory_space=pl.ANY)] * 6,
        out_specs=pl.BlockSpec(memory_space=pltpu.VMEM),
        scratch_shapes=[
            vmem((7, 7, 7, ROWS, MAIN), BF),
            vmem((7, 7, 7, ROWS, TAIL), BF),
            vmem((2, 2, 2, ROWS, MAIN), BF),
            vmem((2, 2, 2, ROWS, TAIL), BF),
            vmem((12, 12, 16, CH), BF),
            vmem((8, 8, 8, CH), BF),
            vmem((6, 6, 4, CH), BF),
            vmem((6, 2, 2, CH), BF),
            vmem((12, 12, 32, MAIN), F32),
            vmem((12, 6, 32, MAIN), F32),
            vmem((8, 2, 48, MAIN), F32),
            vmem((8, 48, MAIN), F32),
            vmem((6, 6, 32, MAIN), F32),
            vmem((6, 3, 32, MAIN), F32),
            vmem((6, 6, 32, MAIN), F32),
            vmem((6, 3, 32, MAIN), F32),
            vmem((9, NBLK, 4, 32, MAIN), BF),
            vmem((2, 9, NBLK, 32, MAIN), BF),
            vmem((9, NBLK, 32, MAIN), BF),
            vmem((2, 9, NBLK, 32, MAIN), BF),
            vmem((7 * 36, ROWS, MAIN), BF),
            vmem((2, ROWS, MAIN), BF),
            vmem((NBLK, 160, MAIN), F32),
            vmem((160, MAIN), F32),
            vmem((160, MAIN), F32),
            vmem((64, 16, MAIN), F32),
            vmem((64, 16, MAIN), F32),
            pltpu.SemaphoreType.DMA((32,)),
            pltpu.SemaphoreType.DMA((6,)),
            pltpu.SemaphoreType.DMA((11,)),
            pltpu.SemaphoreType.DMA((11,)),
        ],
        compiler_params=pltpu.CompilerParams(
            collective_id=0, has_side_effects=True, vmem_limit_bytes=66_000_000
        ),
        name="downward",
    )(multipole_fine, multipole_mid, multipole_coarse, multipole_top, translation_ops, upsample_ops)


def solution(mesh):
    placed = (
        P("space", None, None, None),
        P("space", None, None, None),
        P("space", None, None, None),
        P("space", None, None, None),
        P(),
        P(),
    )
    return jax.shard_map(
        shards,
        mesh=mesh,
        in_specs=placed,
        out_specs=P("space", "level", None, None),
        check_vma=False,
    )
```

```python
import jax
import jax.numpy as jnp
from jax import lax
from jax.experimental import pallas as pl
from jax.experimental.pallas import tpu as pltpu
from jax.sharding import PartitionSpec as P

BF = jnp.bfloat16
F32 = jnp.float32
MESH = pl.DeviceIdType.MESH
CH = 152
MAIN = 128
TAIL = CH - MAIN
ROWS = 160
NBLK = 10


def pad_tail(x):
    zeros = jnp.zeros(x.shape[:-1] + (MAIN - TAIL,), x.dtype)
    return jnp.concatenate([x, zeros], axis=x.ndim - 1)


def kernel(
    mf, mm, mc, mt, tr, up, out,
    tm, tt, um, ut, gb0, gb1, gb2, gb3,
    f0, t0, f1, t1, f2, t2, f3, t3,
    xm, xe, xsm, xse, v, v6, vu, acc, pm, pt, om, ot,
    tsem, gsem, send, recv,
):
    col = lax.axis_index("space")
    lev = lax.axis_index("level")
    n_col = lax.axis_size("space")
    par = col // 2
    base = 2 * par
    odd = lax.rem(col, 2)
    lo_ok = par > 0
    hi_ok = par < n_col // 2 - 1

    barrier = pltpu.get_barrier_semaphore()

    def greet(dev):
        pl.semaphore_signal(barrier, inc=1, device_id=(dev, lev), device_id_type=MESH)

    greet(base + 1 - odd)

    @pl.when(lo_ok)
    def _():
        greet(base - 2)
        greet(base - 1)

    @pl.when(hi_ok)
    def _():
        greet(base + 2)
        greet(base + 3)

    y0 = 6 * lev
    d0 = 2 * (1 - lev)
    y1 = 2 * lev
    loc0 = pltpu.make_async_copy(mf.at[:, pl.ds(y0, 10)], gb0.at[2:10, pl.ds(d0, 10)], gsem.at[0])
    loc1 = pltpu.make_async_copy(mm.at[:, pl.ds(y1, 6)], gb1.at[2:6, pl.ds(d0, 6)], gsem.at[1])
    loc2 = pltpu.make_async_copy(mc, gb2.at[2:4, pl.ds(d0, 4)], gsem.at[2])
    loc3 = pltpu.make_async_copy(mt, gb3.at[3:4], gsem.at[3])
    loc0.start()
    loc1.start()
    loc2.start()
    loc3.start()

    tcopies = {}

    def tcopy(kx, ysl, zsl, i):
        a = pltpu.make_async_copy(
            tr.at[kx, ysl, zsl, :, 0:MAIN], tm.at[kx, ysl, zsl, 0:CH, :], tsem.at[2 * i]
        )
        b = pltpu.make_async_copy(
            tr.at[kx, ysl, zsl, :, MAIN:CH], tt.at[kx, ysl, zsl, 0:CH, :], tsem.at[2 * i + 1]
        )
        a.start()
        b.start()
        tcopies.setdefault(kx, []).extend([a, b])

    idx = 0
    for kx in (3, 2, 4, 1, 0, 5, 6):
        if 2 <= kx <= 4:
            pieces = [
                (slice(0, 2), slice(0, 7)),
                (slice(5, 7), slice(0, 7)),
                (slice(2, 5), slice(0, 2)),
                (slice(2, 5), slice(5, 7)),
            ]
        else:
            pieces = [(slice(0, 7), slice(0, 7))]
        for ysl, zsl in pieces:
            tcopy(kx, ysl, zsl, idx)
            idx += 1
    cu_m = pltpu.make_async_copy(up.at[:, :, :, :, 0:MAIN], um.at[:, :, :, 0:CH, :], gsem.at[4])
    cu_t = pltpu.make_async_copy(up.at[:, :, :, :, MAIN:CH], ut.at[:, :, :, 0:CH, :], gsem.at[5])
    cu_m.start()
    cu_t.start()

    def halo(src, dst, i, dev, j=None):
        return pltpu.make_async_remote_copy(
            src_ref=src, dst_ref=dst, send_sem=send.at[i], recv_sem=recv.at[i if j is None else j],
            device_id=(dev, lev), device_id_type=MESH,
        )

    rights = [
        halo(mf.at[6:8, pl.ds(y0, 10)], gb0.at[0:2, pl.ds(d0, 10)], 0, col + 1),
        halo(mm.at[2:4, pl.ds(y1, 6)], gb1.at[0:2, pl.ds(d0, 6)], 1, col + 1),
        halo(mc, gb2.at[0:2, pl.ds(d0, 4)], 2, col + 1),
    ]
    lefts = [
        halo(mf.at[0:2, pl.ds(y0, 10)], gb0.at[10:12, pl.ds(d0, 10)], 3, col - 1),
        halo(mm.at[0:2, pl.ds(y1, 6)], gb1.at[6:8, pl.ds(d0, 6)], 4, col - 1),
        halo(mc, gb2.at[4:6, pl.ds(d0, 4)], 5, col - 1),
    ]
    top_partner = halo(mt, gb3.at[pl.ds(2 + 2 * odd, 1)], 6, base + 1 - odd)
    top_low = [
        halo(mt, gb3.at[pl.ds(5 + odd - i, 1)], 7 + i, base - 2 + i, 7 + odd) for i in range(2)
    ]
    top_high = [
        halo(mt, gb3.at[pl.ds(1 + odd - i, 1)], 9 + i, base + 2 + i, 9 + odd) for i in range(2)
    ]
    n_greet = 1 + jnp.where(lo_ok, 2, 0) + jnp.where(hi_ok, 2, 0)
    z8 = jnp.zeros((8, MAIN), F32)
    gb0[:, pl.ds(10 * lev, 2)] = jnp.zeros((12, 2, 16, CH), BF)
    gb1[:, pl.ds(6 * lev, 2)] = jnp.zeros((8, 2, 8, CH), BF)
    gb2[:, pl.ds(4 * lev, 2)] = jnp.zeros((6, 2, 4, CH), BF)

    @pl.when(col == 0)
    def _():
        gb0[0:2] = jnp.zeros((2, 12, 16, CH), BF)
        gb1[0:2] = jnp.zeros((2, 8, 8, CH), BF)
        gb2[0:2] = jnp.zeros((2, 6, 4, CH), BF)

    @pl.when(col == n_col - 1)
    def _():
        gb0[10:12] = jnp.zeros((2, 12, 16, CH), BF)
        gb1[6:8] = jnp.zeros((2, 8, 8, CH), BF)
        gb2[4:6] = jnp.zeros((2, 6, 4, CH), BF)

    top0 = jnp.zeros((1, 2, 2, CH), BF)
    gb3[pl.ds(6 * odd, 1)] = top0

    @pl.when(par == 0)
    def _():
        gb3[0:1] = top0
        gb3[1:2] = top0
        gb3[pl.ds(2 * (1 - odd), 1)] = top0

    @pl.when(par == n_col // 2 - 1)
    def _():
        gb3[5:6] = top0
        gb3[6:7] = top0
        gb3[pl.ds(5 - odd, 1)] = top0

    def zero_edges(kx, _):
        for ky in range(7):
            tm[kx, ky, :, CH:ROWS, :] = jnp.zeros((7, ROWS - CH, MAIN), BF)
            tt[kx, ky, :, CH:ROWS, :] = jnp.zeros((7, ROWS - CH, TAIL), BF)
        return 0

    lax.fori_loop(0, 7, zero_edges, 0)

    def zero_near(i, _):
        for kz in range(2, 5):
            tm[2 + i // 3, 2 + lax.rem(i, 3), kz, 0:CH, :] = jnp.zeros((CH, MAIN), BF)
            tt[2 + i // 3, 2 + lax.rem(i, 3), kz, 0:CH, :] = jnp.zeros((CH, TAIL), BF)
        return 0

    lax.fori_loop(0, 9, zero_near, 0)
    um[:, :, :, CH:ROWS, :] = jnp.zeros((2, 2, 2, ROWS - CH, MAIN), BF)
    ut[:, :, :, CH:ROWS, :] = jnp.zeros((2, 2, 2, ROWS - CH, TAIL), BF)

    def zero_pads(x, _):
        for y in range(12):
            f0[x, y, 0:8, :] = z8
            f0[x, y, 24:32, :] = z8
        for yp in range(6):
            t0[x, yp, 0:8, :] = z8
            t0[x, yp, 24:32, :] = z8
        return 0

    lax.fori_loop(0, 12, zero_pads, 0)

    def zero_coarse(x, _):
        f2[x] = jnp.zeros((6, 32, MAIN), F32)
        f3[x] = jnp.zeros((6, 32, MAIN), F32)
        t2[x] = jnp.zeros((3, 32, MAIN), F32)
        t3[x] = jnp.zeros((3, 32, MAIN), F32)
        return 0

    lax.fori_loop(0, 7, zero_coarse, 0)

    def zero_mid(x, _):
        for sy in range(2):
            f1[x, sy, 0:8, :] = z8
            f1[x, sy, 40:48, :] = z8
        t1[x, 0:8, :] = z8
        t1[x, 40:48, :] = z8
        return 0

    lax.fori_loop(0, 8, zero_mid, 0)

    def z_slots(tail, sy):
        even = lax.rem(lax.broadcasted_iota(jnp.int32, tail.shape, 0), 2) == 0
        a = pltpu.roll(tail, 64 * sy, 1) if sy else tail
        b = pltpu.roll(tail, 64 * sy + 32, 1)
        return jnp.where(even, a, b)

    def conv0(x):
        for yp in range(6):
            tails = []
            for sy in range(2):
                y = 2 * yp + sy
                f0[x, y, 8:24, :] = gb0[x, y, :, 0:MAIN].astype(F32)
                tails.append(z_slots(pad_tail(gb0[x, y, :, MAIN:CH].astype(F32)), sy))
            t0[x, yp, 8:24, :] = tails[0] + tails[1]

    def build0(xp, w, store):
        sty, stz = (w // 3, w % 3) if isinstance(w, int) else (w // 3, lax.rem(w, 3))
        for sx in range(2):
            x = 2 * xp + sx
            for sy in range(2):
                for sz in range(2):
                    rows = [
                        f0[x, 2 * (py + sty) + sy, pl.ds(6 + 2 * stz + sz, 8, stride=2), :]
                        for py in range(4)
                    ]
                    store(w, 4 * sx + 2 * sy + sz, jnp.concatenate(rows, axis=0).astype(BF))
            rows = [
                t0[x, py + sty, pl.ds(6 + 2 * stz, 8, stride=2), :]
                + t0[x, py + sty, pl.ds(7 + 2 * stz, 8, stride=2), :]
                for py in range(4)
            ]
            store(w, 8 + sx, jnp.concatenate(rows, axis=0).astype(BF))

    with jax.named_scope("conv_own"):
        loc0.wait()

        def own_conv(x, _):
            conv0(x)
            return 0

        lax.fori_loop(2, 10, own_conv, 0)

    with jax.named_scope("build_own"):

        def own_build(w, _):
            for xp in range(1, 5):

                def store(w, j, val, xp=xp):
                    xm[w, j, xp - 1] = val

                build0(xp, w, store)
            return 0

        lax.fori_loop(0, 9, own_build, 0)

    with jax.named_scope("greet"):
        pl.semaphore_wait(barrier, n_greet)

        top_partner.start()

        @pl.when(lo_ok)
        def _():
            for c in top_low:
                c.start()

        @pl.when(hi_ok)
        def _():
            for c in top_high:
                c.start()

        @pl.when(col < n_col - 1)
        def _():
            for c in rights[::-1]:
                c.start()

        @pl.when(col > 0)
        def _():
            for c in lefts[::-1]:
                c.start()

    def conv1(x):
        for yp in range(4):
            tails = []
            for sy in range(2):
                y = 2 * yp + sy
                f1[x, sy, 8 + 8 * yp : 16 + 8 * yp, :] = gb1[x, y, :, 0:MAIN].astype(F32)
                tails.append(z_slots(pad_tail(gb1[x, y, :, MAIN:CH].astype(F32)), sy))
            t1[x, 8 + 8 * yp : 16 + 8 * yp, :] = tails[0] + tails[1]

    def conv2(x):
        for yp in range(3):
            tails = []
            for sy in range(2):
                y = 2 * yp + sy
                f2[x, y, 8:12, :] = gb2[x, y, :, 0:MAIN].astype(F32)
                tails.append(z_slots(pad_tail(gb2[x, y, :, MAIN:CH].astype(F32)), sy))
            t2[x, yp, 8:12, :] = tails[0] + tails[1]

    def conv3(x):
        tails = []
        for y in range(2):
            f3[x, 2 + y, 8:10, :] = gb3[x, y, :, 0:MAIN].astype(F32)
            tails.append(z_slots(pad_tail(gb3[x, y, :, MAIN:CH].astype(F32)), y))
        t3[x, 1, 8:10, :] = tails[0] + tails[1]

    with jax.named_scope("conv_small"):
        loc1.wait()
        loc2.wait()
        loc3.wait()
        for x in range(2, 6):
            conv1(x)
        for x in range(2, 4):
            conv2(x)
        conv3(3)

    def build_small(stx, sty, stz, store):
        row = lax.broadcasted_iota(jnp.int32, (8, MAIN), 0)
        pz = lax.rem(row, 4) + stz - 1
        inside = (pz >= 0) & (pz < 4)

        def put(j, one, two, three, four):
            one = [jnp.where(inside, p, 0.0) for p in one]
            rest = jnp.where(row < 2, two, 0.0)
            if three is not None:
                rest = jnp.where(row == 2, three, rest)
            if four is not None:
                rest = jnp.where(row == 3, four, rest)
            store(3 * sty + stz, j, jnp.concatenate(one + [rest, z8], axis=0).astype(BF))

        for sx in range(2):
            three_x = {0: (1, 2), 1: (3, None), 2: (None, 6)}[stx][sx]
            four_x = {0: (0, None), 1: (None, None), 2: (4, 5)}[stx][sx]

            def top(x, y, start):
                if x is None:
                    return None
                return f3[x, y, pl.ds(start + 2 * stz, 8, stride=2), :]

            def top_tail(x, start):
                if x is None:
                    return None
                return (
                    t3[x, sty, pl.ds(start + 2 * stz, 8, stride=2), :]
                    + t3[x, sty, pl.ds(start + 1 + 2 * stz, 8, stride=2), :]
                )

            for sy in range(2):
                for sz in range(2):
                    one = [
                        f1[2 * (px + stx) + sx, sy, pl.ds(6 + 8 * sty + 2 * stz + sz, 8, stride=2), :]
                        for px in range(2)
                    ]
                    y = 2 * sty + sy
                    two = f2[2 * stx + sx, y, pl.ds(6 + 2 * stz + sz, 8, stride=2), :]
                    three = top(three_x, y, 2 + sz)
                    four = top(four_x, y, sz)
                    put(4 * sx + 2 * sy + sz, one, two, three, four)
            one = [
                t1[2 * (px + stx) + sx, pl.ds(6 + 8 * sty + 2 * stz, 8, stride=2), :]
                + t1[2 * (px + stx) + sx, pl.ds(7 + 8 * sty + 2 * stz, 8, stride=2), :]
                for px in range(2)
            ]
            two = (
                t2[2 * stx + sx, sty, pl.ds(6 + 2 * stz, 8, stride=2), :]
                + t2[2 * stx + sx, sty, pl.ds(7 + 2 * stz, 8, stride=2), :]
            )
            put(8 + sx, one, two, top_tail(three_x, 2), top_tail(four_x, 0))

    with jax.named_scope("build_small"):

        def small_mid(sty, _):
            def store(w, j, val):
                xsm[w, j] = val

            for stz in range(3):
                build_small(1, sty, stz, store)
            return 0

        lax.fori_loop(0, 3, small_mid, 0)

    def tail_unit(kx, rz):
        last = None
        for ky in range(7):
            a = pad_tail(tt[kx, ky, rz + 1])
            b = pad_tail(tt[kx, ky, rz])
            pair = a + pltpu.roll(b, 32, 1)
            if last is not None:
                if kx == 6:
                    v6[(ky - 1) * 6 + rz] = pair + last
                else:
                    v[(kx * 6 + ky - 1) * 6 + rz] = pair + last
            last = pltpu.roll(pair, 64, 1)

    def lhs_of(stx, sty, stzs):
        parts = []
        for stz in stzs:
            w = 3 * sty + stz
            for j in range(NBLK):
                if stx == 1:
                    rows = [xm[w, j].reshape(128, MAIN), xsm[w, j]]
                elif stx == 0:
                    rows = [xe[0, w, j], xm[w, j, 0:3].reshape(96, MAIN), xse[0, w, j]]
                else:
                    rows = [xm[w, j, 1:4].reshape(96, MAIN), xe[1, w, j], xse[1, w, j]]
                parts.append(jnp.concatenate(rows, axis=0))
        return jnp.concatenate(parts, axis=1)

    def dot_n(n, stx, sty, stzs):
        blocks = []
        for stz in stzs:
            mains = []
            tails = []
            for s in range(8):
                sx, sy, sz = s >> 2, (s >> 1) & 1, s & 1
                pair = []
                for h in range(2):
                    if n < 4:
                        c = 2 * n + h
                        kx = 2 * stx + sx - (c >> 2) + 1
                        ky = 2 * sty + sy - ((c >> 1) & 1) + 1
                        kz = 2 * stz + sz - (c & 1) + 1
                        pair.append((tm[kx, ky, kz, 0:MAIN, :], tm[kx, ky, kz, MAIN:ROWS, :]))
                    else:
                        kx = 2 * stx + sx - h + 1
                        ref = v6 if kx == 6 else v
                        k = ((0 if kx == 6 else 6 * kx) + 2 * sty + sy) * 6 + 2 * stz + sz
                        pair.append((ref[k, 0:MAIN, :], ref[k, MAIN:ROWS, :]))
                mains.append(jnp.concatenate([p[0] for p in pair], axis=1))
                tails.append(jnp.concatenate([p[1] for p in pair], axis=1))
            blocks += mains + tails
        rhs = jnp.concatenate(blocks, axis=0)
        res = jnp.dot(lhs_of(stx, sty, stzs), rhs, preferred_element_type=F32)
        acc[2 * n] += res[:, 0:MAIN]
        acc[2 * n + 1] += res[:, MAIN:]

    def block(stx, sty, stzs, fill):
        for n in range(4):
            dot_n(n, stx, sty, stzs)
            for k in range(n * len(fill) // 4, (n + 1) * len(fill) // 4):
                fill[k]()

    def wait_t(*slabs):
        for kx in slabs:
            for c in tcopies[kx]:
                c.wait()

    acc[...] = jnp.zeros(acc.shape, F32)
    with jax.named_scope("wait_t"):
        wait_t(3)
    with jax.named_scope("front"):

        def front(rz, _):
            tail_unit(3, rz)
            return 0

        lax.fori_loop(2, 6, front, 0)
    with jax.named_scope("wait_t"):
        wait_t(2, 4)
    with jax.named_scope("mxu1"):

        def body(i, _):
            units = [lambda q=q: tail_unit(2, 3 * i + q) for q in range(3)]
            units.append(lambda: tail_unit(3, i))
            block(1, 2 * i, (0, 1, 2), units)
            return 0

        lax.fori_loop(0, 2, body, 0)

    with jax.named_scope("wait_halo"):
        @pl.when(col > 0)
        def _():
            for c in rights:
                c.wait_recv()

        @pl.when(col < n_col - 1)
        def _():
            for c in lefts:
                c.wait_recv()

        halo(mt, gb3.at[pl.ds(4 - 2 * odd, 1)], 6, base + 1 - odd).wait_recv()

        @pl.when(lo_ok)
        def _():
            for i in range(2):
                halo(mt, gb3.at[pl.ds(1 + i - odd, 1)], 9 + i, base - 2 + i).wait_recv()

        @pl.when(hi_ok)
        def _():
            for i in range(2):
                halo(mt, gb3.at[pl.ds(5 + i - odd, 1)], 7 + i, base + 2 + i).wait_recv()

    with jax.named_scope("mxu1c"):
        fill = [lambda x=x: conv0(x) for x in (0, 1, 10, 11)]
        fill += [lambda x=x: conv1(x) for x in (0, 1, 6, 7)]
        fill += [lambda x=x: conv2(x) for x in (0, 1, 4, 5)]
        fill += [lambda x=x: conv3(x) for x in (0, 1, 2, 4, 5, 6)]
        for w in range(9):
            for side in range(2):

                def edge(w=w, side=side):
                    def store(w, j, val):
                        xe[side, w, j] = val

                    build0(5 * side, w, store)

                def small(w=w, side=side):
                    def store(w, j, val):
                        xse[side, w, j] = val

                    build_small(2 * side, w // 3, w % 3, store)

                fill += [edge, small]
        block(1, 1, (0, 2), fill)
    for stx, slabs, extra in ((0, (1, 0), (4, 1)), (2, (5, 6), (0, 5))):
        with jax.named_scope("wait_t"):
            wait_t(*slabs)
        with jax.named_scope("mxu02"):

            def body(sty, _, stx=stx, extra=extra):
                units = [
                    lambda kx=kx, q=q: tail_unit(kx, 2 * sty + q) for q in range(2) for kx in extra
                ]
                block(stx, sty, (0, 1, 2), units)
                return 0

            lax.fori_loop(0, 3, body, 0)
    with jax.named_scope("mxu_tail"):
        for stx, first in ((1, 0), (0, 3), (2, None)):

            def body(sty, _, stx=stx, first=first):
                dot_n(4, stx, sty, (0, 1, 2))
                if first is not None:
                    tail_unit(6, first + sty)
                return 0

            lax.fori_loop(0, 3, body, 0)

    cu_m.wait()
    cu_t.wait()
    for h in range(2):
        parts = [pad_tail(ut[h, q >> 1, q & 1]) for q in range(4)]
        total = parts[0]
        for q in range(1, 4):
            total = total + pltpu.roll(parts[q], 32 * q, 1)
        vu[h] = total

    def upsampled(main, tail):
        rows = main.shape[0]
        hi_m = main.astype(BF)
        lo_m = (main - hi_m.astype(F32)).astype(BF)
        hi_t = tail.astype(BF).astype(F32)
        both = (hi_t + pltpu.roll(tail - hi_t, 32, 1)).astype(BF)
        lhs = jnp.concatenate([hi_m, lo_m, both], axis=1)

        def rhs_of(x):
            return jnp.concatenate(
                [x(0, MAIN), x(0, MAIN), x(MAIN, ROWS), x(MAIN, ROWS), jnp.zeros((64, MAIN), BF)],
                axis=0,
            )

        cols = []
        for n in range(5):
            if n < 4:
                pair = [
                    rhs_of(lambda lo, hi, c=c: um[c >> 2, (c >> 1) & 1, c & 1, lo:hi, :])
                    for c in (2 * n, 2 * n + 1)
                ]
            else:
                pair = [rhs_of(lambda lo, hi, h=h: vu[h, lo:hi, :]) for h in range(2)]
            res = jnp.dot(lhs, jnp.concatenate(pair, axis=1), preferred_element_type=F32)
            cols += [res[:, 0:MAIN], res[:, MAIN:]]
        return cols

    def tail_lanes(x, c):
        q = c & 3
        y = pltpu.roll(x, MAIN - 32 * q, 1) if q else x
        lane = lax.broadcasted_iota(jnp.int32, x.shape, 1)
        return jnp.where(lane < TAIL, y, 0.0)

    pm[...] = jnp.zeros(pm.shape, F32)
    pt[...] = jnp.zeros(pt.shape, F32)
    rest = [acc[j, 144:152, :] for j in range(NBLK)]
    for cz in range(2):
        mains = []
        tails = []
        for cy in range(2):
            c = 2 * cy + cz
            mains.append(rest[c][2:3] + rest[4 + c][3:4])
            tails.append(tail_lanes(rest[8], c)[2:3] + tail_lanes(rest[9], c)[3:4])
        pm[cz : cz + 1, :] = jnp.where(lev == 0, mains[0], mains[1])
        pt[cz : cz + 1, :] = jnp.where(lev == 0, tails[0], tails[1])
    add = upsampled(pm[0:16, :], pt[0:16, :])
    local2 = [rest[j] + add[j][0:8] for j in range(NBLK)]
    for c in range(8):
        cx, cy, cz = c >> 2, (c >> 1) & 1, c & 1
        tail = tail_lanes(local2[8 + cx], c)
        for p in range(2):
            r = 8 * cx + 4 * cy + 2 * p + cz
            pm[16 + r : 17 + r, :] = local2[c][p : p + 1]
            pt[16 + r : 17 + r, :] = tail[p : p + 1]
    add = upsampled(pm[16:32, :], pt[16:32, :])
    local1 = [acc[j, 128:144, :] + add[j] for j in range(NBLK)]
    for c in range(8):
        cx, cy, cz = c >> 2, (c >> 1) & 1, c & 1
        tail = tail_lanes(local1[8 + cx], c)
        for px in range(2):
            for py in range(2):
                r = 32 + 32 * (2 * px + cx) + 8 * (2 * py + cy) + cz
                q = 8 * px + 4 * py
                pm[pl.ds(r, 4, stride=2), :] = local1[c][q : q + 4]
                pt[pl.ds(r, 4, stride=2), :] = tail[q : q + 4]
    add = upsampled(pm[32:160, :], pt[32:160, :])
    for c in range(8):
        cx, cy, cz = c >> 2, (c >> 1) & 1, c & 1
        main = acc[c, 0:128, :] + add[c]
        tail = tail_lanes(acc[8 + cx, 0:128, :] + add[8 + cx], c)
        for px in range(4):
            for py in range(4):
                q = 32 * px + 8 * py
                x, y = 2 * px + cx, 2 * py + cy
                om[8 * x + y, pl.ds(cz, 8, stride=2), :] = main[q : q + 8]
                ot[8 * x + y, pl.ds(cz, 8, stride=2), :] = tail[q : q + 8]

    def emit(x, _):
        for y in range(8):
            out[x, y, :, 0:MAIN] = om[8 * x + y]
            out[x, y, :, MAIN:CH] = ot[8 * x + y][:, 0:TAIL]
        return 0

    lax.fori_loop(0, 8, emit, 0)

    top_partner.wait_send()

    @pl.when(lo_ok)
    def _():
        for c in top_low:
            c.wait_send()

    @pl.when(hi_ok)
    def _():
        for c in top_high:
            c.wait_send()

    @pl.when(col < n_col - 1)
    def _():
        for c in rights:
            c.wait_send()

    @pl.when(col > 0)
    def _():
        for c in lefts:
            c.wait_send()


def shards(
    multipole_fine, multipole_mid, multipole_coarse, multipole_top, translation_ops, upsample_ops
):
    vmem = pltpu.VMEM
    return pl.pallas_call(
        kernel,
        out_shape=jax.ShapeDtypeStruct((8, 8, 16, CH), F32),
        in_specs=[pl.BlockSpec(memory_space=pl.ANY)] * 6,
        out_specs=pl.BlockSpec(memory_space=pltpu.VMEM),
        scratch_shapes=[
            vmem((7, 7, 7, ROWS, MAIN), BF),
            vmem((7, 7, 7, ROWS, TAIL), BF),
            vmem((2, 2, 2, ROWS, MAIN), BF),
            vmem((2, 2, 2, ROWS, TAIL), BF),
            vmem((12, 12, 16, CH), BF),
            vmem((8, 8, 8, CH), BF),
            vmem((6, 6, 4, CH), BF),
            vmem((7, 2, 2, CH), BF),
            vmem((12, 12, 32, MAIN), F32),
            vmem((12, 6, 32, MAIN), F32),
            vmem((8, 2, 48, MAIN), F32),
            vmem((8, 48, MAIN), F32),
            vmem((7, 6, 32, MAIN), F32),
            vmem((7, 3, 32, MAIN), F32),
            vmem((7, 6, 32, MAIN), F32),
            vmem((7, 3, 32, MAIN), F32),
            vmem((9, NBLK, 4, 32, MAIN), BF),
            vmem((2, 9, NBLK, 32, MAIN), BF),
            vmem((9, NBLK, 32, MAIN), BF),
            vmem((2, 9, NBLK, 32, MAIN), BF),
            vmem((6 * 36, ROWS, MAIN), BF),
            vmem((36, ROWS, MAIN), BF),
            vmem((2, ROWS, MAIN), BF),
            vmem((NBLK, 160, MAIN), F32),
            vmem((160, MAIN), F32),
            vmem((160, MAIN), F32),
            vmem((64, 16, MAIN), F32),
            vmem((64, 16, MAIN), F32),
            pltpu.SemaphoreType.DMA((32,)),
            pltpu.SemaphoreType.DMA((6,)),
            pltpu.SemaphoreType.DMA((11,)),
            pltpu.SemaphoreType.DMA((11,)),
        ],
        compiler_params=pltpu.CompilerParams(
            collective_id=0, has_side_effects=True, vmem_limit_bytes=66_000_000
        ),
        name="downward",
    )(multipole_fine, multipole_mid, multipole_coarse, multipole_top, translation_ops, upsample_ops)


def solution(mesh):
    placed = (
        P("space", None, None, None),
        P("space", None, None, None),
        P("space", None, None, None),
        P("space", None, None, None),
        P(),
        P(),
    )
    return jax.shard_map(
        shards,
        mesh=mesh,
        in_specs=placed,
        out_specs=P("space", "level", None, None),
        check_vma=False,
    )
```

```python
import jax
import jax.numpy as jnp
from jax import lax
from jax.experimental import pallas as pl
from jax.experimental.pallas import tpu as pltpu
from jax.sharding import PartitionSpec as P

BF = jnp.bfloat16
F32 = jnp.float32
MESH = pl.DeviceIdType.MESH
CH = 152
MAIN = 128
TAIL = CH - MAIN
ROWS = 160
NBLK = 10


def pad_tail(x):
    zeros = jnp.zeros(x.shape[:-1] + (MAIN - TAIL,), x.dtype)
    return jnp.concatenate([x, zeros], axis=x.ndim - 1)


def kernel(
    mf, mm, mc, mt, tr, out,
    tm, tt, gb0, gb1, gb2, gb3,
    f0, t0, f1, t1, f2, t2, f3, t3,
    xm, xl, xr, xsm, xsl, xsr, v, v6, acc,
    tsem, gsem, send, recv,
):
    col = lax.axis_index("space")
    lev = lax.axis_index("level")
    n_col = lax.axis_size("space")
    par = col // 2
    base = 2 * par
    odd = lax.rem(col, 2)
    lo_ok = par > 0
    hi_ok = par < n_col // 2 - 1

    barrier = pltpu.get_barrier_semaphore()

    def greet(dev):
        pl.semaphore_signal(barrier, inc=1, device_id=(dev, lev), device_id_type=MESH)

    greet(base + 1 - odd)

    @pl.when(lo_ok)
    def _():
        greet(base - 2)
        greet(base - 1)

    @pl.when(hi_ok)
    def _():
        greet(base + 2)
        greet(base + 3)

    y0 = 6 * lev
    d0 = 2 * (1 - lev)
    y1 = 2 * lev
    loc0 = pltpu.make_async_copy(mf.at[:, pl.ds(y0, 10)], gb0.at[2:10, pl.ds(d0, 10)], gsem.at[0])
    loc1 = pltpu.make_async_copy(mm.at[:, pl.ds(y1, 6)], gb1.at[2:6, pl.ds(d0, 6)], gsem.at[1])
    loc2 = pltpu.make_async_copy(mc, gb2.at[2:4, pl.ds(d0, 4)], gsem.at[2])
    loc3 = pltpu.make_async_copy(mt, gb3.at[3:4], gsem.at[3])
    loc0.start()
    loc1.start()
    loc2.start()
    loc3.start()

    tcopies = {}

    def tcopy(kx, ysl, zsl, i):
        a = pltpu.make_async_copy(
            tr.at[kx, ysl, zsl, :, 0:MAIN], tm.at[kx, ysl, zsl, 0:CH, :], tsem.at[2 * i]
        )
        b = pltpu.make_async_copy(
            tr.at[kx, ysl, zsl, :, MAIN:CH], tt.at[kx, ysl, zsl, 0:CH, :], tsem.at[2 * i + 1]
        )
        a.start()
        b.start()
        tcopies.setdefault(kx, []).extend([a, b])

    idx = 0
    for kx in (3, 2, 4, 1, 0, 5, 6):
        if 2 <= kx <= 4:
            pieces = [
                (slice(0, 2), slice(0, 7)),
                (slice(5, 7), slice(0, 7)),
                (slice(2, 5), slice(0, 2)),
                (slice(2, 5), slice(5, 7)),
            ]
        else:
            pieces = [(slice(0, 7), slice(0, 7))]
        for ysl, zsl in pieces:
            tcopy(kx, ysl, zsl, idx)
            idx += 1
    def halo(src, dst, i, dev, j=None):
        return pltpu.make_async_remote_copy(
            src_ref=src, dst_ref=dst, send_sem=send.at[i], recv_sem=recv.at[i if j is None else j],
            device_id=(dev, lev), device_id_type=MESH,
        )

    rights = [
        halo(mf.at[6:8, pl.ds(y0, 10)], gb0.at[0:2, pl.ds(d0, 10)], 0, col + 1),
        halo(mm.at[2:4, pl.ds(y1, 6)], gb1.at[0:2, pl.ds(d0, 6)], 1, col + 1),
        halo(mc, gb2.at[0:2, pl.ds(d0, 4)], 2, col + 1),
    ]
    lefts = [
        halo(mf.at[0:2, pl.ds(y0, 10)], gb0.at[10:12, pl.ds(d0, 10)], 3, col - 1),
        halo(mm.at[0:2, pl.ds(y1, 6)], gb1.at[6:8, pl.ds(d0, 6)], 4, col - 1),
        halo(mc, gb2.at[4:6, pl.ds(d0, 4)], 5, col - 1),
    ]
    top_partner = halo(mt, gb3.at[pl.ds(2 + 2 * odd, 1)], 6, base + 1 - odd)
    top_low = [
        halo(mt, gb3.at[pl.ds(5 + odd - i, 1)], 7 + i, base - 2 + i, 7 + odd) for i in range(2)
    ]
    top_high = [
        halo(mt, gb3.at[pl.ds(1 + odd - i, 1)], 9 + i, base + 2 + i, 9 + odd) for i in range(2)
    ]
    n_greet = 1 + jnp.where(lo_ok, 2, 0) + jnp.where(hi_ok, 2, 0)
    z8 = jnp.zeros((8, MAIN), F32)
    gb0[:, pl.ds(10 * lev, 2)] = jnp.zeros((12, 2, 16, CH), BF)
    gb1[:, pl.ds(6 * lev, 2)] = jnp.zeros((8, 2, 8, CH), BF)
    gb2[:, pl.ds(4 * lev, 2)] = jnp.zeros((6, 2, 4, CH), BF)

    @pl.when(col == 0)
    def _():
        gb0[0:2] = jnp.zeros((2, 12, 16, CH), BF)
        gb1[0:2] = jnp.zeros((2, 8, 8, CH), BF)
        gb2[0:2] = jnp.zeros((2, 6, 4, CH), BF)

    @pl.when(col == n_col - 1)
    def _():
        gb0[10:12] = jnp.zeros((2, 12, 16, CH), BF)
        gb1[6:8] = jnp.zeros((2, 8, 8, CH), BF)
        gb2[4:6] = jnp.zeros((2, 6, 4, CH), BF)

    top0 = jnp.zeros((1, 2, 2, CH), BF)
    gb3[pl.ds(6 * odd, 1)] = top0

    @pl.when(par == 0)
    def _():
        gb3[0:1] = top0
        gb3[1:2] = top0
        gb3[pl.ds(2 * (1 - odd), 1)] = top0

    @pl.when(par == n_col // 2 - 1)
    def _():
        gb3[5:6] = top0
        gb3[6:7] = top0
        gb3[pl.ds(5 - odd, 1)] = top0

    def zero_edges(kx, _):
        for ky in range(7):
            tm[kx, ky, :, CH:ROWS, :] = jnp.zeros((7, ROWS - CH, MAIN), BF)
            tt[kx, ky, :, CH:ROWS, :] = jnp.zeros((7, ROWS - CH, TAIL), BF)
        return 0

    lax.fori_loop(0, 7, zero_edges, 0)

    def zero_near(i, _):
        for kz in range(2, 5):
            tm[2 + i // 3, 2 + lax.rem(i, 3), kz, 0:CH, :] = jnp.zeros((CH, MAIN), BF)
            tt[2 + i // 3, 2 + lax.rem(i, 3), kz, 0:CH, :] = jnp.zeros((CH, TAIL), BF)
        return 0

    lax.fori_loop(0, 9, zero_near, 0)
    def zero_pads(x, _):
        for y in range(12):
            f0[x, y, 0:8, :] = z8
            f0[x, y, 24:32, :] = z8
        for yp in range(6):
            t0[x, yp, 0:8, :] = z8
            t0[x, yp, 24:32, :] = z8
        return 0

    lax.fori_loop(0, 12, zero_pads, 0)

    def zero_coarse(x, _):
        f2[x] = jnp.zeros((6, 32, MAIN), F32)
        f3[x] = jnp.zeros((6, 32, MAIN), F32)
        t2[x] = jnp.zeros((3, 32, MAIN), F32)
        t3[x] = jnp.zeros((3, 32, MAIN), F32)
        return 0

    lax.fori_loop(0, 7, zero_coarse, 0)

    def zero_mid(x, _):
        for sy in range(2):
            f1[x, sy, 0:8, :] = z8
            f1[x, sy, 40:48, :] = z8
        t1[x, 0:8, :] = z8
        t1[x, 40:48, :] = z8
        return 0

    lax.fori_loop(0, 8, zero_mid, 0)

    def z_slots(tail, sy):
        even = lax.rem(lax.broadcasted_iota(jnp.int32, tail.shape, 0), 2) == 0
        a = pltpu.roll(tail, 64 * sy, 1) if sy else tail
        b = pltpu.roll(tail, 64 * sy + 32, 1)
        return jnp.where(even, a, b)

    def conv0(x):
        for yp in range(6):
            tails = []
            for sy in range(2):
                y = 2 * yp + sy
                f0[x, y, 8:24, :] = gb0[x, y, :, 0:MAIN].astype(F32)
                tails.append(z_slots(pad_tail(gb0[x, y, :, MAIN:CH].astype(F32)), sy))
            t0[x, yp, 8:24, :] = tails[0] + tails[1]

    def build0(xp, w, store):
        sty, stz = (w // 3, w % 3) if isinstance(w, int) else (w // 3, lax.rem(w, 3))
        for sx in range(2):
            x = 2 * xp + sx
            for sy in range(2):
                for sz in range(2):
                    rows = [
                        f0[x, 2 * (py + sty) + sy, pl.ds(6 + 2 * stz + sz, 8, stride=2), :]
                        for py in range(4)
                    ]
                    store(w, 4 * sx + 2 * sy + sz, jnp.concatenate(rows, axis=0).astype(BF))
            rows = [
                t0[x, py + sty, pl.ds(6 + 2 * stz, 8, stride=2), :]
                + t0[x, py + sty, pl.ds(7 + 2 * stz, 8, stride=2), :]
                for py in range(4)
            ]
            store(w, 8 + sx, jnp.concatenate(rows, axis=0).astype(BF))

    with jax.named_scope("conv_own"):
        loc0.wait()

        def own_conv(x, _):
            conv0(x)
            return 0

        lax.fori_loop(2, 10, own_conv, 0)

    with jax.named_scope("build_own"):

        def own_build(w, _):
            for xp in range(1, 5):

                def store(w, j, val, xp=xp):
                    xm[w, j, xp - 1] = val

                build0(xp, w, store)
            return 0

        lax.fori_loop(0, 9, own_build, 0)

    with jax.named_scope("greet"):
        pl.semaphore_wait(barrier, n_greet)

        top_partner.start()

        @pl.when(lo_ok)
        def _():
            for c in top_low:
                c.start()

        @pl.when(hi_ok)
        def _():
            for c in top_high:
                c.start()

        @pl.when(col < n_col - 1)
        def _():
            for c in rights[::-1]:
                c.start()

        @pl.when(col > 0)
        def _():
            for c in lefts[::-1]:
                c.start()

    def conv1(x):
        for yp in range(4):
            tails = []
            for sy in range(2):
                y = 2 * yp + sy
                f1[x, sy, 8 + 8 * yp : 16 + 8 * yp, :] = gb1[x, y, :, 0:MAIN].astype(F32)
                tails.append(z_slots(pad_tail(gb1[x, y, :, MAIN:CH].astype(F32)), sy))
            t1[x, 8 + 8 * yp : 16 + 8 * yp, :] = tails[0] + tails[1]

    def conv2(x):
        for yp in range(3):
            tails = []
            for sy in range(2):
                y = 2 * yp + sy
                f2[x, y, 8:12, :] = gb2[x, y, :, 0:MAIN].astype(F32)
                tails.append(z_slots(pad_tail(gb2[x, y, :, MAIN:CH].astype(F32)), sy))
            t2[x, yp, 8:12, :] = tails[0] + tails[1]

    def conv3(x):
        tails = []
        for y in range(2):
            f3[x, 2 + y, 8:10, :] = gb3[x, y, :, 0:MAIN].astype(F32)
            tails.append(z_slots(pad_tail(gb3[x, y, :, MAIN:CH].astype(F32)), y))
        t3[x, 1, 8:10, :] = tails[0] + tails[1]

    with jax.named_scope("conv_small"):
        loc1.wait()
        loc2.wait()
        loc3.wait()
        for x in range(2, 6):
            conv1(x)
        for x in range(2, 4):
            conv2(x)
        conv3(3)

    def build_small(stx, sty, stz, store):
        row = lax.broadcasted_iota(jnp.int32, (8, MAIN), 0)
        pz = lax.rem(row, 4) + stz - 1
        inside = (pz >= 0) & (pz < 4)

        def put(j, one, two, three, four):
            one = [jnp.where(inside, p, 0.0) for p in one]
            rest = jnp.where(row < 2, two, 0.0)
            if three is not None:
                rest = jnp.where(row == 2, three, rest)
            if four is not None:
                rest = jnp.where(row == 3, four, rest)
            store(3 * sty + stz, j, jnp.concatenate(one + [rest, z8], axis=0).astype(BF))

        for sx in range(2):
            three_x = {0: (1, 2), 1: (3, None), 2: (None, 6)}[stx][sx]
            four_x = {0: (0, None), 1: (None, None), 2: (4, 5)}[stx][sx]

            def top(x, y, start):
                if x is None:
                    return None
                return f3[x, y, pl.ds(start + 2 * stz, 8, stride=2), :]

            def top_tail(x, start):
                if x is None:
                    return None
                return (
                    t3[x, sty, pl.ds(start + 2 * stz, 8, stride=2), :]
                    + t3[x, sty, pl.ds(start + 1 + 2 * stz, 8, stride=2), :]
                )

            for sy in range(2):
                for sz in range(2):
                    one = [
                        f1[2 * (px + stx) + sx, sy, pl.ds(6 + 8 * sty + 2 * stz + sz, 8, stride=2), :]
                        for px in range(2)
                    ]
                    y = 2 * sty + sy
                    two = f2[2 * stx + sx, y, pl.ds(6 + 2 * stz + sz, 8, stride=2), :]
                    three = top(three_x, y, 2 + sz)
                    four = top(four_x, y, sz)
                    put(4 * sx + 2 * sy + sz, one, two, three, four)
            one = [
                t1[2 * (px + stx) + sx, pl.ds(6 + 8 * sty + 2 * stz, 8, stride=2), :]
                + t1[2 * (px + stx) + sx, pl.ds(7 + 8 * sty + 2 * stz, 8, stride=2), :]
                for px in range(2)
            ]
            two = (
                t2[2 * stx + sx, sty, pl.ds(6 + 2 * stz, 8, stride=2), :]
                + t2[2 * stx + sx, sty, pl.ds(7 + 2 * stz, 8, stride=2), :]
            )
            put(8 + sx, one, two, top_tail(three_x, 2), top_tail(four_x, 0))

    with jax.named_scope("build_small"):

        def small_mid(sty, _):
            def store(w, j, val):
                xsm[w, j] = val

            for stz in range(3):
                build_small(1, sty, stz, store)
            return 0

        lax.fori_loop(0, 3, small_mid, 0)

    def tail_unit(kx, rz):
        last = None
        for ky in range(7):
            a = pad_tail(tt[kx, ky, rz + 1])
            b = pad_tail(tt[kx, ky, rz])
            pair = a + pltpu.roll(b, 32, 1)
            if last is not None:
                if kx == 6:
                    v6[(ky - 1) * 6 + rz] = pair + last
                else:
                    v[(kx * 6 + ky - 1) * 6 + rz] = pair + last
            last = pltpu.roll(pair, 64, 1)

    def lhs_of(stx, sty, stzs):
        parts = []
        for stz in stzs:
            w = 3 * sty + stz
            for j in range(NBLK):
                if stx == 1:
                    rows = [xm[w, j].reshape(128, MAIN), xsm[w, j]]
                elif stx == 0:
                    rows = [xl[w, j], xm[w, j, 0:3].reshape(96, MAIN), xsl[w, j]]
                else:
                    rows = [xm[w, j, 1:4].reshape(96, MAIN), xr[w, j], xsr[w, j]]
                parts.append(jnp.concatenate(rows, axis=0))
        return jnp.concatenate(parts, axis=1)

    def dot_n(n, stx, sty, stzs):
        blocks = []
        for stz in stzs:
            mains = []
            tails = []
            for s in range(8):
                sx, sy, sz = s >> 2, (s >> 1) & 1, s & 1
                pair = []
                for h in range(2):
                    if n < 4:
                        c = 2 * n + h
                        kx = 2 * stx + sx - (c >> 2) + 1
                        ky = 2 * sty + sy - ((c >> 1) & 1) + 1
                        kz = 2 * stz + sz - (c & 1) + 1
                        pair.append((tm[kx, ky, kz, 0:MAIN, :], tm[kx, ky, kz, MAIN:ROWS, :]))
                    else:
                        kx = 2 * stx + sx - h + 1
                        ref = v6 if kx == 6 else v
                        k = ((0 if kx == 6 else 6 * kx) + 2 * sty + sy) * 6 + 2 * stz + sz
                        pair.append((ref[k, 0:MAIN, :], ref[k, MAIN:ROWS, :]))
                mains.append(jnp.concatenate([p[0] for p in pair], axis=1))
                tails.append(jnp.concatenate([p[1] for p in pair], axis=1))
            blocks += mains + tails
        rhs = jnp.concatenate(blocks, axis=0)
        res = jnp.dot(lhs_of(stx, sty, stzs), rhs, preferred_element_type=F32)
        acc[2 * n] += res[:, 0:MAIN]
        acc[2 * n + 1] += res[:, MAIN:]

    def block(stx, sty, stzs, fill):
        for n in range(4):
            dot_n(n, stx, sty, stzs)
            for k in range(n * len(fill) // 4, (n + 1) * len(fill) // 4):
                fill[k]()

    def wait_t(*slabs):
        for kx in slabs:
            for c in tcopies[kx]:
                c.wait()

    acc[...] = jnp.zeros(acc.shape, F32)
    with jax.named_scope("wait_t"):
        wait_t(3)
    with jax.named_scope("front"):

        def front(rz, _):
            tail_unit(3, rz)
            return 0

        lax.fori_loop(0, 6, front, 0)
    with jax.named_scope("wait_t"):
        wait_t(2, 4)
    with jax.named_scope("mxu1"):

        def body(i, _):
            units = [lambda q=q: tail_unit(2, 3 * i + q) for q in range(3)]
            units.append(lambda: tail_unit(4, i))
            block(1, 2 * i, (0, 1, 2), units)
            return 0

        lax.fori_loop(0, 2, body, 0)
    with jax.named_scope("mxu1c"):
        block(1, 1, (0, 2), [lambda q=q: tail_unit(4, q) for q in range(2, 6)])

    def tail_dots(stx):
        def body(sty, _):
            dot_n(4, stx, sty, (0, 1, 2))
            return 0

        with jax.named_scope("mxu_tail"):
            lax.fori_loop(0, 3, body, 0)

    tail_dots(1)

    with jax.named_scope("wait_halo"):
        @pl.when(col > 0)
        def _():
            for c in rights:
                c.wait_recv()

        @pl.when(col < n_col - 1)
        def _():
            for c in lefts:
                c.wait_recv()

        halo(mt, gb3.at[pl.ds(4 - 2 * odd, 1)], 6, base + 1 - odd).wait_recv()

        @pl.when(lo_ok)
        def _():
            for i in range(2):
                halo(mt, gb3.at[pl.ds(1 + i - odd, 1)], 9 + i, base - 2 + i).wait_recv()

        @pl.when(hi_ok)
        def _():
            for i in range(2):
                halo(mt, gb3.at[pl.ds(5 + i - odd, 1)], 7 + i, base + 2 + i).wait_recv()

    def edge(w, side):
        def store(w, j, val):
            (xl, xr)[side][w, j] = val

        def store_small(w, j, val):
            (xsl, xsr)[side][w, j] = val

        build0(5 * side, w, store)
        if isinstance(w, int):
            build_small(2 * side, w // 3, w % 3, store_small)
        else:
            build_small(2 * side, w // 3, lax.rem(w, 3), store_small)

    with jax.named_scope("edges"):
        for x in (0, 1, 10, 11):
            conv0(x)
        for x in (0, 1, 6, 7):
            conv1(x)
        for x in (0, 1, 4, 5):
            conv2(x)
        for x in (0, 1, 2, 4, 5, 6):
            conv3(x)

        def left_edge(sty, _):
            for q in range(3):
                edge(3 * sty + q, 0)
            return 0

        lax.fori_loop(0, 3, left_edge, 0)
    with jax.named_scope("wait_t"):
        wait_t(1, 0)
    with jax.named_scope("mxu02"):

        def body(sty, _):
            units = []
            for q in range(2):
                units.append(lambda q=q: tail_unit(1, 2 * sty + q))
                units.append(lambda q=q: tail_unit(0, 2 * sty + q))
            fill = []
            for q in range(3):
                fill.append(lambda q=q: edge(3 * sty + q, 1))
            block(0, sty, (0, 1, 2), [units[0], fill[0], units[1], fill[1], units[2], fill[2], units[3]])
            return 0

        lax.fori_loop(0, 3, body, 0)
    with jax.named_scope("wait_t"):
        wait_t(5, 6)
    with jax.named_scope("mxu02"):

        def body(sty, _):
            units = [lambda kx=kx, q=q: tail_unit(kx, 2 * sty + q) for q in range(2) for kx in (5, 6)]
            block(2, sty, (0, 1, 2), units)
            return 0

        lax.fori_loop(0, 3, body, 0)

    done_main = pltpu.make_async_copy(acc.at[0:8], out.at[0:8], gsem.at[0])
    done_main.start()
    tail_dots(0)
    tail_dots(2)
    done_tail = pltpu.make_async_copy(acc.at[8:NBLK], out.at[8:NBLK], gsem.at[1])
    done_tail.start()
    done_main.wait()
    done_tail.wait()

    top_partner.wait_send()

    @pl.when(lo_ok)
    def _():
        for c in top_low:
            c.wait_send()

    @pl.when(hi_ok)
    def _():
        for c in top_high:
            c.wait_send()

    @pl.when(col < n_col - 1)
    def _():
        for c in rights:
            c.wait_send()

    @pl.when(col > 0)
    def _():
        for c in lefts:
            c.wait_send()


def finish(acc, up, out, vu, pm, pt, om, ot):
    lev = lax.axis_index("level")

    def up_rows(c, lo, hi, lane):
        return up[c >> 2, (c >> 1) & 1, c & 1, lo:hi, lane]

    for h in range(2):
        parts = [pad_tail(up[h, q >> 1, q & 1, :, MAIN:CH]) for q in range(4)]
        total = parts[0]
        for q in range(1, 4):
            total = total + pltpu.roll(parts[q], 32 * q, 1)
        vu[h, 0:CH, :] = total
        vu[h, CH:ROWS, :] = jnp.zeros((ROWS - CH, MAIN), BF)

    def upsampled(main, tail):
        rows = main.shape[0]
        hi_m = main.astype(BF)
        lo_m = (main - hi_m.astype(F32)).astype(BF)
        hi_t = tail.astype(BF).astype(F32)
        both = (hi_t + pltpu.roll(tail - hi_t, 32, 1)).astype(BF)
        lhs = jnp.concatenate([hi_m, lo_m, both], axis=1)

        def rhs_of(main, last):
            last = jnp.concatenate([last, jnp.zeros((ROWS - CH, MAIN), BF)], axis=0)
            return jnp.concatenate([main, main, last, last, jnp.zeros((64, MAIN), BF)], axis=0)

        cols = []
        for n in range(5):
            if n < 4:
                pair = [
                    rhs_of(up_rows(c, 0, MAIN, slice(0, MAIN)), up_rows(c, MAIN, CH, slice(0, MAIN)))
                    for c in (2 * n, 2 * n + 1)
                ]
            else:
                pair = [rhs_of(vu[h, 0:MAIN, :], vu[h, MAIN:CH, :]) for h in range(2)]
            res = jnp.dot(lhs, jnp.concatenate(pair, axis=1), preferred_element_type=F32)
            cols += [res[:, 0:MAIN], res[:, MAIN:]]
        return cols

    def tail_lanes(x, c):
        q = c & 3
        y = pltpu.roll(x, MAIN - 32 * q, 1) if q else x
        lane = lax.broadcasted_iota(jnp.int32, x.shape, 1)
        return jnp.where(lane < TAIL, y, 0.0)

    pm[...] = jnp.zeros(pm.shape, F32)
    pt[...] = jnp.zeros(pt.shape, F32)
    rest = [acc[j, 144:152, :] for j in range(NBLK)]
    for cz in range(2):
        mains = []
        tails = []
        for cy in range(2):
            c = 2 * cy + cz
            mains.append(rest[c][2:3] + rest[4 + c][3:4])
            tails.append(tail_lanes(rest[8], c)[2:3] + tail_lanes(rest[9], c)[3:4])
        pm[cz : cz + 1, :] = jnp.where(lev == 0, mains[0], mains[1])
        pt[cz : cz + 1, :] = jnp.where(lev == 0, tails[0], tails[1])
    add = upsampled(pm[0:16, :], pt[0:16, :])
    local2 = [rest[j] + add[j][0:8] for j in range(NBLK)]
    for c in range(8):
        cx, cy, cz = c >> 2, (c >> 1) & 1, c & 1
        tail = tail_lanes(local2[8 + cx], c)
        for p in range(2):
            r = 8 * cx + 4 * cy + 2 * p + cz
            pm[16 + r : 17 + r, :] = local2[c][p : p + 1]
            pt[16 + r : 17 + r, :] = tail[p : p + 1]
    add = upsampled(pm[16:32, :], pt[16:32, :])
    local1 = [acc[j, 128:144, :] + add[j] for j in range(NBLK)]
    for c in range(8):
        cx, cy, cz = c >> 2, (c >> 1) & 1, c & 1
        tail = tail_lanes(local1[8 + cx], c)
        for px in range(2):
            for py in range(2):
                r = 32 + 32 * (2 * px + cx) + 8 * (2 * py + cy) + cz
                q = 8 * px + 4 * py
                pm[pl.ds(r, 4, stride=2), :] = local1[c][q : q + 4]
                pt[pl.ds(r, 4, stride=2), :] = tail[q : q + 4]
    add = upsampled(pm[32:160, :], pt[32:160, :])
    for px in range(4):
        own = slice(32 * px, 32 * px + 32)
        for c in range(8):
            cx, cy, cz = c >> 2, (c >> 1) & 1, c & 1
            main = acc[c, own, :] + add[c][own]
            tail = tail_lanes(acc[8 + cx, own, :] + add[8 + cx][own], c)
            for py in range(4):
                q = 8 * py
                x, y = 2 * px + cx, 2 * py + cy
                om[8 * x + y, pl.ds(cz, 8, stride=2), :] = main[q : q + 8]
                ot[8 * x + y, pl.ds(cz, 8, stride=2), :] = tail[q : q + 8]
        for x in (2 * px, 2 * px + 1):
            for y in range(8):
                out[x, y, :, 0:MAIN] = om[8 * x + y]
                out[x, y, :, MAIN:CH] = ot[8 * x + y][:, 0:TAIL]


def shards(
    multipole_fine, multipole_mid, multipole_coarse, multipole_top, translation_ops, upsample_ops
):
    vmem = pltpu.VMEM
    far = pl.pallas_call(
        kernel,
        out_shape=jax.ShapeDtypeStruct((NBLK, 160, MAIN), F32),
        in_specs=[pl.BlockSpec(memory_space=pl.ANY)] * 5,
        out_specs=pl.BlockSpec(memory_space=pl.ANY),
        scratch_shapes=[
            vmem((7, 7, 7, ROWS, MAIN), BF),
            vmem((7, 7, 7, ROWS, TAIL), BF),
            vmem((12, 12, 16, CH), BF),
            vmem((8, 8, 8, CH), BF),
            vmem((6, 6, 4, CH), BF),
            vmem((7, 2, 2, CH), BF),
            vmem((12, 12, 32, MAIN), F32),
            vmem((12, 6, 32, MAIN), F32),
            vmem((8, 2, 48, MAIN), F32),
            vmem((8, 48, MAIN), F32),
            vmem((7, 6, 32, MAIN), F32),
            vmem((7, 3, 32, MAIN), F32),
            vmem((7, 6, 32, MAIN), F32),
            vmem((7, 3, 32, MAIN), F32),
            vmem((9, NBLK, 4, 32, MAIN), BF),
            vmem((9, NBLK, 32, MAIN), BF),
            vmem((9, NBLK, 32, MAIN), BF),
            vmem((9, NBLK, 32, MAIN), BF),
            vmem((9, NBLK, 32, MAIN), BF),
            vmem((9, NBLK, 32, MAIN), BF),
            vmem((6 * 36, ROWS, MAIN), BF),
            vmem((36, ROWS, MAIN), BF),
            vmem((NBLK, 160, MAIN), F32),
            pltpu.SemaphoreType.DMA((32,)),
            pltpu.SemaphoreType.DMA((6,)),
            pltpu.SemaphoreType.DMA((11,)),
            pltpu.SemaphoreType.DMA((11,)),
        ],
        compiler_params=pltpu.CompilerParams(
            collective_id=0, has_side_effects=True, vmem_limit_bytes=66_000_000
        ),
        name="downward",
    )(multipole_fine, multipole_mid, multipole_coarse, multipole_top, translation_ops)
    return pl.pallas_call(
        finish,
        out_shape=jax.ShapeDtypeStruct((8, 8, 16, CH), F32),
        in_specs=[pl.BlockSpec(memory_space=pltpu.VMEM)] * 2,
        out_specs=pl.BlockSpec(memory_space=pltpu.VMEM),
        scratch_shapes=[
            vmem((2, ROWS, MAIN), BF),
            vmem((160, MAIN), F32),
            vmem((160, MAIN), F32),
            vmem((64, 16, MAIN), F32),
            vmem((64, 16, MAIN), F32),
        ],
        name="upsample",
    )(far, upsample_ops)


def solution(mesh):
    placed = (
        P("space", None, None, None),
        P("space", None, None, None),
        P("space", None, None, None),
        P("space", None, None, None),
        P(),
        P(),
    )
    return jax.shard_map(
        shards,
        mesh=mesh,
        in_specs=placed,
        out_specs=P("space", "level", None, None),
        check_vma=False,
    )
```

```python
import jax
import jax.numpy as jnp
from jax import lax
from jax.experimental import pallas as pl
from jax.experimental.pallas import tpu as pltpu
from jax.sharding import PartitionSpec as P

BF = jnp.bfloat16
F32 = jnp.float32
MESH = pl.DeviceIdType.MESH
CH = 152
MAIN = 128
TAIL = CH - MAIN
ROWS = 160
NBLK = 10


def pad_tail(x):
    zeros = jnp.zeros(x.shape[:-1] + (MAIN - TAIL,), x.dtype)
    return jnp.concatenate([x, zeros], axis=x.ndim - 1)


def kernel(
    mf, mm, mc, mt, tr, acc,
    tm, tt, gb0, gb1, gb2, gb3,
    f0, t0, f1, t1, f2, t2, f3, t3,
    xm, xl, xr, xsm, xsl, xsr, v,
    tsem, gsem, send, recv,
):
    col = lax.axis_index("space")
    lev = lax.axis_index("level")
    n_col = lax.axis_size("space")
    par = col // 2
    base = 2 * par
    odd = lax.rem(col, 2)
    lo_ok = par > 0
    hi_ok = par < n_col // 2 - 1

    barrier = pltpu.get_barrier_semaphore()

    def greet(dev):
        pl.semaphore_signal(barrier, inc=1, device_id=(dev, lev), device_id_type=MESH)

    greet(base + 1 - odd)

    @pl.when(lo_ok)
    def _():
        greet(base - 2)
        greet(base - 1)

    @pl.when(hi_ok)
    def _():
        greet(base + 2)
        greet(base + 3)

    y0 = 6 * lev
    d0 = 2 * (1 - lev)
    y1 = 2 * lev
    loc0 = pltpu.make_async_copy(mf.at[:, pl.ds(y0, 10)], gb0.at[2:10, pl.ds(d0, 10)], gsem.at[0])
    loc1 = pltpu.make_async_copy(mm.at[:, pl.ds(y1, 6)], gb1.at[2:6, pl.ds(d0, 6)], gsem.at[1])
    loc2 = pltpu.make_async_copy(mc, gb2.at[2:4, pl.ds(d0, 4)], gsem.at[2])
    loc3 = pltpu.make_async_copy(mt, gb3.at[3:4], gsem.at[3])
    loc0.start()
    loc1.start()
    loc2.start()
    loc3.start()

    tcopies = {}

    def tcopy(kx, ysl, zsl, i):
        a = pltpu.make_async_copy(
            tr.at[kx, ysl, zsl, :, 0:MAIN], tm.at[kx, ysl, zsl, 0:CH, :], tsem.at[2 * i]
        )
        b = pltpu.make_async_copy(
            tr.at[kx, ysl, zsl, :, MAIN:CH], tt.at[kx, ysl, zsl, 0:CH, :], tsem.at[2 * i + 1]
        )
        a.start()
        b.start()
        tcopies.setdefault(kx, []).extend([a, b])

    idx = 0
    for kx in (3, 2, 4, 1, 0, 5, 6):
        if 2 <= kx <= 4:
            pieces = [
                (slice(0, 2), slice(0, 7)),
                (slice(5, 7), slice(0, 7)),
                (slice(2, 5), slice(0, 2)),
                (slice(2, 5), slice(5, 7)),
            ]
        else:
            pieces = [(slice(0, 7), slice(0, 7))]
        for ysl, zsl in pieces:
            tcopy(kx, ysl, zsl, idx)
            idx += 1
    def halo(src, dst, i, dev, j=None):
        return pltpu.make_async_remote_copy(
            src_ref=src, dst_ref=dst, send_sem=send.at[i], recv_sem=recv.at[i if j is None else j],
            device_id=(dev, lev), device_id_type=MESH,
        )

    rights = [
        halo(mf.at[6:8, pl.ds(y0, 10)], gb0.at[0:2, pl.ds(d0, 10)], 0, col + 1),
        halo(mm.at[2:4, pl.ds(y1, 6)], gb1.at[0:2, pl.ds(d0, 6)], 1, col + 1),
        halo(mc, gb2.at[0:2, pl.ds(d0, 4)], 2, col + 1),
    ]
    lefts = [
        halo(mf.at[0:2, pl.ds(y0, 10)], gb0.at[10:12, pl.ds(d0, 10)], 3, col - 1),
        halo(mm.at[0:2, pl.ds(y1, 6)], gb1.at[6:8, pl.ds(d0, 6)], 4, col - 1),
        halo(mc, gb2.at[4:6, pl.ds(d0, 4)], 5, col - 1),
    ]
    top_partner = halo(mt, gb3.at[pl.ds(2 + 2 * odd, 1)], 6, base + 1 - odd)
    top_low = [
        halo(mt, gb3.at[pl.ds(5 + odd - i, 1)], 7 + i, base - 2 + i, 7 + odd) for i in range(2)
    ]
    top_high = [
        halo(mt, gb3.at[pl.ds(1 + odd - i, 1)], 9 + i, base + 2 + i, 9 + odd) for i in range(2)
    ]
    n_greet = 1 + jnp.where(lo_ok, 2, 0) + jnp.where(hi_ok, 2, 0)
    z8 = jnp.zeros((8, MAIN), F32)
    gb0[:, pl.ds(10 * lev, 2)] = jnp.zeros((12, 2, 16, CH), BF)
    gb1[:, pl.ds(6 * lev, 2)] = jnp.zeros((8, 2, 8, CH), BF)
    gb2[:, pl.ds(4 * lev, 2)] = jnp.zeros((6, 2, 4, CH), BF)

    @pl.when(col == 0)
    def _():
        gb0[0:2] = jnp.zeros((2, 12, 16, CH), BF)
        gb1[0:2] = jnp.zeros((2, 8, 8, CH), BF)
        gb2[0:2] = jnp.zeros((2, 6, 4, CH), BF)

    @pl.when(col == n_col - 1)
    def _():
        gb0[10:12] = jnp.zeros((2, 12, 16, CH), BF)
        gb1[6:8] = jnp.zeros((2, 8, 8, CH), BF)
        gb2[4:6] = jnp.zeros((2, 6, 4, CH), BF)

    top0 = jnp.zeros((1, 2, 2, CH), BF)
    gb3[pl.ds(6 * odd, 1)] = top0

    @pl.when(par == 0)
    def _():
        gb3[0:1] = top0
        gb3[1:2] = top0
        gb3[pl.ds(2 * (1 - odd), 1)] = top0

    @pl.when(par == n_col // 2 - 1)
    def _():
        gb3[5:6] = top0
        gb3[6:7] = top0
        gb3[pl.ds(5 - odd, 1)] = top0

    def zero_edges(kx, _):
        for ky in range(7):
            tm[kx, ky, :, CH:ROWS, :] = jnp.zeros((7, ROWS - CH, MAIN), BF)
            tt[kx, ky, :, CH:ROWS, :] = jnp.zeros((7, ROWS - CH, TAIL), BF)
        return 0

    lax.fori_loop(0, 7, zero_edges, 0)

    def zero_near(i, _):
        for kz in range(2, 5):
            tm[2 + i // 3, 2 + lax.rem(i, 3), kz, 0:CH, :] = jnp.zeros((CH, MAIN), BF)
            tt[2 + i // 3, 2 + lax.rem(i, 3), kz, 0:CH, :] = jnp.zeros((CH, TAIL), BF)
        return 0

    lax.fori_loop(0, 9, zero_near, 0)
    def zero_pads(x, _):
        for y in range(12):
            f0[x, y, 0:8, :] = z8
            f0[x, y, 24:32, :] = z8
        for yp in range(6):
            t0[x, yp, 0:8, :] = z8
            t0[x, yp, 24:32, :] = z8
        return 0

    lax.fori_loop(0, 12, zero_pads, 0)

    def zero_coarse(x, _):
        f2[x] = jnp.zeros((6, 32, MAIN), F32)
        f3[x] = jnp.zeros((6, 32, MAIN), F32)
        t2[x] = jnp.zeros((3, 32, MAIN), F32)
        t3[x] = jnp.zeros((3, 32, MAIN), F32)
        return 0

    lax.fori_loop(0, 7, zero_coarse, 0)

    def zero_mid(x, _):
        for sy in range(2):
            f1[x, sy, 0:8, :] = z8
            f1[x, sy, 40:48, :] = z8
        t1[x, 0:8, :] = z8
        t1[x, 40:48, :] = z8
        return 0

    lax.fori_loop(0, 8, zero_mid, 0)

    def z_slots(tail, sy):
        even = lax.rem(lax.broadcasted_iota(jnp.int32, tail.shape, 0), 2) == 0
        a = pltpu.roll(tail, 64 * sy, 1) if sy else tail
        b = pltpu.roll(tail, 64 * sy + 32, 1)
        return jnp.where(even, a, b)

    def conv0(x):
        for yp in range(6):
            tails = []
            for sy in range(2):
                y = 2 * yp + sy
                f0[x, y, 8:24, :] = gb0[x, y, :, 0:MAIN].astype(F32)
                tails.append(z_slots(pad_tail(gb0[x, y, :, MAIN:CH].astype(F32)), sy))
            t0[x, yp, 8:24, :] = tails[0] + tails[1]

    def build0(xp, w, store):
        sty, stz = (w // 3, w % 3) if isinstance(w, int) else (w // 3, lax.rem(w, 3))
        for sx in range(2):
            x = 2 * xp + sx
            for sy in range(2):
                for sz in range(2):
                    rows = [
                        f0[x, 2 * (py + sty) + sy, pl.ds(6 + 2 * stz + sz, 8, stride=2), :]
                        for py in range(4)
                    ]
                    store(w, 4 * sx + 2 * sy + sz, jnp.concatenate(rows, axis=0).astype(BF))
            rows = [
                t0[x, py + sty, pl.ds(6 + 2 * stz, 8, stride=2), :]
                + t0[x, py + sty, pl.ds(7 + 2 * stz, 8, stride=2), :]
                for py in range(4)
            ]
            store(w, 8 + sx, jnp.concatenate(rows, axis=0).astype(BF))

    with jax.named_scope("conv_own"):
        loc0.wait()

        def own_conv(x, _):
            conv0(x)
            return 0

        lax.fori_loop(2, 10, own_conv, 0)

    with jax.named_scope("build_own"):

        def own_build(w, _):
            for xp in range(1, 5):

                def store(w, j, val, xp=xp):
                    xm[w, j, xp - 1] = val

                build0(xp, w, store)
            return 0

        lax.fori_loop(0, 9, own_build, 0)

    def conv1(x):
        for yp in range(4):
            tails = []
            for sy in range(2):
                y = 2 * yp + sy
                f1[x, sy, 8 + 8 * yp : 16 + 8 * yp, :] = gb1[x, y, :, 0:MAIN].astype(F32)
                tails.append(z_slots(pad_tail(gb1[x, y, :, MAIN:CH].astype(F32)), sy))
            t1[x, 8 + 8 * yp : 16 + 8 * yp, :] = tails[0] + tails[1]

    def conv2(x):
        for yp in range(3):
            tails = []
            for sy in range(2):
                y = 2 * yp + sy
                f2[x, y, 8:12, :] = gb2[x, y, :, 0:MAIN].astype(F32)
                tails.append(z_slots(pad_tail(gb2[x, y, :, MAIN:CH].astype(F32)), sy))
            t2[x, yp, 8:12, :] = tails[0] + tails[1]

    def conv3(x):
        tails = []
        for y in range(2):
            f3[x, 2 + y, 8:10, :] = gb3[x, y, :, 0:MAIN].astype(F32)
            tails.append(z_slots(pad_tail(gb3[x, y, :, MAIN:CH].astype(F32)), y))
        t3[x, 1, 8:10, :] = tails[0] + tails[1]

    with jax.named_scope("conv_small"):
        loc1.wait()
        loc2.wait()
        loc3.wait()
        for x in range(2, 6):
            conv1(x)
        for x in range(2, 4):
            conv2(x)
        conv3(3)

    def build_small(stx, sty, stz, store):
        row = lax.broadcasted_iota(jnp.int32, (8, MAIN), 0)
        pz = lax.rem(row, 4) + stz - 1
        inside = (pz >= 0) & (pz < 4)

        def put(j, one, two, three, four):
            one = [jnp.where(inside, p, 0.0) for p in one]
            rest = jnp.where(row < 2, two, 0.0)
            if three is not None:
                rest = jnp.where(row == 2, three, rest)
            if four is not None:
                rest = jnp.where(row == 3, four, rest)
            store(3 * sty + stz, j, jnp.concatenate(one + [rest, z8], axis=0).astype(BF))

        for sx in range(2):
            if isinstance(stx, int):
                three_x, four_x = ((3, None)[sx], None)
                keep = None
            else:
                three_x = 1 if sx == 0 else 2 + 2 * stx
                four_x = 2 * stx if sx == 0 else 5
                keep = (stx == 0) if sx == 0 else (stx == 2)

            def only(val, wanted):
                return val if keep is None or not wanted else jnp.where(keep, val, 0.0)

            def top(x, y, start, wanted):
                if x is None:
                    return None
                return only(f3[x, y, pl.ds(start + 2 * stz, 8, stride=2), :], wanted)

            def top_tail(x, start, wanted):
                if x is None:
                    return None
                return only(
                    t3[x, sty, pl.ds(start + 2 * stz, 8, stride=2), :]
                    + t3[x, sty, pl.ds(start + 1 + 2 * stz, 8, stride=2), :],
                    wanted,
                )

            for sy in range(2):
                for sz in range(2):
                    one = [
                        f1[2 * (px + stx) + sx, sy, pl.ds(6 + 8 * sty + 2 * stz + sz, 8, stride=2), :]
                        for px in range(2)
                    ]
                    y = 2 * sty + sy
                    two = f2[2 * stx + sx, y, pl.ds(6 + 2 * stz + sz, 8, stride=2), :]
                    three = top(three_x, y, 2 + sz, sx == 0)
                    four = top(four_x, y, sz, sx == 1)
                    put(4 * sx + 2 * sy + sz, one, two, three, four)
            one = [
                t1[2 * (px + stx) + sx, pl.ds(6 + 8 * sty + 2 * stz, 8, stride=2), :]
                + t1[2 * (px + stx) + sx, pl.ds(7 + 8 * sty + 2 * stz, 8, stride=2), :]
                for px in range(2)
            ]
            two = (
                t2[2 * stx + sx, sty, pl.ds(6 + 2 * stz, 8, stride=2), :]
                + t2[2 * stx + sx, sty, pl.ds(7 + 2 * stz, 8, stride=2), :]
            )
            put(8 + sx, one, two, top_tail(three_x, 2, sx == 0), top_tail(four_x, 0, sx == 1))

    with jax.named_scope("build_small"):

        def small_mid(sty, _):
            def store(w, j, val):
                xsm[w, j] = val

            for stz in range(3):
                build_small(1, sty, stz, store)
            return 0

        lax.fori_loop(0, 3, small_mid, 0)

    def tail_unit(kx, rz):
        last = None
        for ky in range(7):
            a = pad_tail(tt[kx, ky, rz + 1])
            b = pad_tail(tt[kx, ky, rz])
            pair = a + pltpu.roll(b, 32, 1)
            if last is not None:
                v[(kx * 6 + ky - 1) * 6 + rz] = pair + last
            last = pltpu.roll(pair, 64, 1)

    def wait_t(*slabs):
        for kx in slabs:
            for c in tcopies[kx]:
                c.wait()

    with jax.named_scope("wait_t"):
        wait_t(3)
    with jax.named_scope("front"):

        def front(rz, _):
            tail_unit(3, rz)
            return 0

        pass
    with jax.named_scope("greet"):
        pl.semaphore_wait(barrier, n_greet)

        top_partner.start()

        @pl.when(lo_ok)
        def _():
            for c in top_low:
                c.start()

        @pl.when(hi_ok)
        def _():
            for c in top_high:
                c.start()

        @pl.when((col < n_col - 1) & (lev == 0))
        def _():
            for c in rights[::-1]:
                c.start()

        @pl.when((col > 0) & (lev == 1))
        def _():
            for c in lefts[::-1]:
                c.start()

    def lhs_of(stx, sty, stzs):
        parts = []
        for stz in stzs:
            w = 3 * sty + stz
            for j in range(NBLK):
                if stx == 1:
                    rows = [xm[w, j].reshape(128, MAIN), xsm[w, j]]
                elif isinstance(stx, tuple):
                    k, side = stx
                    mid = xm[w, j, pl.ds(side, 3)].reshape(96, MAIN)
                    rows = [(xl, xr)[k][w, j], mid, (xsl, xsr)[k][w, j]]
                parts.append(jnp.concatenate(rows, axis=0))
        return jnp.concatenate(parts, axis=1)

    def dot_n(n, stx, sty, stzs):
        blocks = []
        lhs = lhs_of(stx, sty, stzs)
        two_sided = isinstance(stx, tuple)
        if two_sided:
            side = stx[1]
            stx = 2 * side
        for stz in stzs:
            mains = []
            tails = []
            for s in range(8):
                sx, sy, sz = s >> 2, (s >> 1) & 1, s & 1
                pair = []
                for h in range(2):
                    if n < 4:
                        c = 2 * n + h
                        kx = 2 * stx + sx - (c >> 2) + 1
                        ky = 2 * sty + sy - ((c >> 1) & 1) + 1
                        kz = 2 * stz + sz - (c & 1) + 1
                        pair.append((tm[kx, ky, kz, 0:MAIN, :], tm[kx, ky, kz, MAIN:ROWS, :]))
                    else:
                        k = ((2 * stx + sx - h + 1) * 6 + 2 * sty + sy) * 6 + 2 * stz + sz
                        pair.append((v[k, 0:MAIN, :], v[k, MAIN:ROWS, :]))
                mains.append(jnp.concatenate([p[0] for p in pair], axis=1))
                tails.append(jnp.concatenate([p[1] for p in pair], axis=1))
            blocks += mains + tails
        rhs = jnp.concatenate(blocks, axis=0)
        res = jnp.dot(lhs, rhs, preferred_element_type=F32)
        for h in range(2):
            own = res[:, MAIN * h : MAIN * (h + 1)]
            if two_sided:
                acc[2 * n + h, pl.ds(pl.multiple_of(96 * side, 32), 32)] += own[0:32]
                acc[2 * n + h, pl.ds(pl.multiple_of(32 - 32 * side, 32), 96)] += own[32:128]
                acc[2 * n + h, 128:160] += own[128:160]
            else:
                acc[2 * n + h] += own

    def block(stx, sty, stzs, fill):
        for n in range(4):
            dot_n(n, stx, sty, stzs)
            for k in range(n * len(fill) // 4, (n + 1) * len(fill) // 4):
                fill[k]()

    with jax.named_scope("front"):
        lax.fori_loop(0, 6, front, 0)
    acc[...] = jnp.zeros(acc.shape, F32)
    with jax.named_scope("wait_t"):
        wait_t(2, 4)
    with jax.named_scope("mxu1"):

        def body(i, _):
            units = [lambda q=q: tail_unit(2, 3 * i + q) for q in range(3)]
            units.append(lambda: tail_unit(4, i))
            block(1, 2 * i, (0, 1, 2), units)
            return 0

        lax.fori_loop(0, 2, body, 0)

    @pl.when((col < n_col - 1) & (lev == 1))
    def _():
        for c in rights[::-1]:
            c.start()

    @pl.when((col > 0) & (lev == 0))
    def _():
        for c in lefts[::-1]:
            c.start()

    with jax.named_scope("mxu1c"):
        block(1, 1, (0, 2), [lambda q=q: tail_unit(4, q) for q in range(2, 6)])

    def tail_dots(stx):
        def body(sty, _):
            dot_n(4, stx, sty, (0, 1, 2))
            return 0

        with jax.named_scope("mxu_tail"):
            lax.fori_loop(0, 3, body, 0)

    tail_dots(1)

    with jax.named_scope("wait_halo"):

        halo(mt, gb3.at[pl.ds(4 - 2 * odd, 1)], 6, base + 1 - odd).wait_recv()

        @pl.when(lo_ok)
        def _():
            for i in range(2):
                halo(mt, gb3.at[pl.ds(1 + i - odd, 1)], 9 + i, base - 2 + i).wait_recv()

        @pl.when(hi_ok)
        def _():
            for i in range(2):
                halo(mt, gb3.at[pl.ds(5 + i - odd, 1)], 7 + i, base + 2 + i).wait_recv()

        @pl.when((col > 0) & (lev == 0))
        def _():
            for c in rights:
                c.wait_recv()

        @pl.when((col < n_col - 1) & (lev == 1))
        def _():
            for c in lefts:
                c.wait_recv()

    one_side = lev
    two_side = 1 - lev

    def convert(side):
        for x in range(2):
            conv0(10 * side + x)
            conv1(6 * side + x)
            conv2(4 * side + x)
        for x in range(3):
            conv3(4 * side + x)

    def edge(w, side, k):
        def store(w, j, val):
            (xl, xr)[k][w, j] = val

        def store_small(w, j, val):
            (xsl, xsr)[k][w, j] = val

        build0(5 * side, w, store)
        build_small(2 * side, w // 3, lax.rem(w, 3), store_small)

    with jax.named_scope("edges"):
        convert(one_side)

        def first_edge(sty, _):
            for q in range(3):
                edge(3 * sty + q, one_side, 0)
            return 0

        lax.fori_loop(0, 3, first_edge, 0)
    with jax.named_scope("wait_t"):
        wait_t(1, 0, 5, 6)

    def units_of(sty, slabs):
        return [lambda kx=kx, q=q: tail_unit(kx, 2 * sty + q) for q in range(2) for kx in slabs]

    def side_body(k, side, more):
        def body(sty, _):
            fill = units_of(sty, (1, 0) if k == 0 else (5, 6))
            for q in range(more):
                fill.append(lambda q=q: edge(more * sty - more + q, two_side, 1))
            block((k, side), sty, (0, 1, 2), fill)
            return 0

        return body

    with jax.named_scope("mxu02"):
        lax.fori_loop(0, 1, side_body(0, one_side, 0), 0)
    with jax.named_scope("wait_halo"):

        @pl.when((col > 0) & (lev == 1))
        def _():
            for c in rights:
                c.wait_recv()

        @pl.when((col < n_col - 1) & (lev == 0))
        def _():
            for c in lefts:
                c.wait_recv()

    with jax.named_scope("edges"):
        convert(two_side)
    with jax.named_scope("mxu02"):
        lax.fori_loop(1, 3, side_body(0, one_side, 4), 0)
    edge(jnp.int32(8), two_side, 1)
    with jax.named_scope("mxu02"):
        lax.fori_loop(0, 3, side_body(1, two_side, 0), 0)

    tail_dots((0, one_side))
    tail_dots((1, two_side))

    top_partner.wait_send()

    @pl.when(lo_ok)
    def _():
        for c in top_low:
            c.wait_send()

    @pl.when(hi_ok)
    def _():
        for c in top_high:
            c.wait_send()

    @pl.when(col < n_col - 1)
    def _():
        for c in rights:
            c.wait_send()

    @pl.when(col > 0)
    def _():
        for c in lefts:
            c.wait_send()


def finish(acc, up, out, vu, pm, pt, om, ot, ob, osem):
    lev = lax.axis_index("level")
    def up_rows(c, lo, hi, lane):
        return up[c >> 2, (c >> 1) & 1, c & 1, lo:hi, lane]

    for h in range(2):
        parts = [pad_tail(up[h, q >> 1, q & 1, :, MAIN:CH]) for q in range(4)]
        total = parts[0]
        for q in range(1, 4):
            total = total + pltpu.roll(parts[q], 32 * q, 1)
        vu[h, 0:CH, :] = total
        vu[h, CH:ROWS, :] = jnp.zeros((ROWS - CH, MAIN), BF)

    def upsampled(main, tail):
        rows = main.shape[0]
        hi_m = main.astype(BF)
        lo_m = (main - hi_m.astype(F32)).astype(BF)
        hi_t = tail.astype(BF).astype(F32)
        both = (hi_t + pltpu.roll(tail - hi_t, 32, 1)).astype(BF)
        lhs = jnp.concatenate([hi_m, lo_m, both], axis=1)

        def rhs_of(main, last):
            last = jnp.concatenate([last, jnp.zeros((ROWS - CH, MAIN), BF)], axis=0)
            return jnp.concatenate([main, main, last, last, jnp.zeros((64, MAIN), BF)], axis=0)

        cols = []
        for n in range(5):
            if n < 4:
                pair = [
                    rhs_of(up_rows(c, 0, MAIN, slice(0, MAIN)), up_rows(c, MAIN, CH, slice(0, MAIN)))
                    for c in (2 * n, 2 * n + 1)
                ]
            else:
                pair = [rhs_of(vu[h, 0:MAIN, :], vu[h, MAIN:CH, :]) for h in range(2)]
            res = jnp.dot(lhs, jnp.concatenate(pair, axis=1), preferred_element_type=F32)
            cols += [res[:, 0:MAIN], res[:, MAIN:]]
        return cols

    def tail_lanes(x, c):
        q = c & 3
        y = pltpu.roll(x, MAIN - 32 * q, 1) if q else x
        lane = lax.broadcasted_iota(jnp.int32, x.shape, 1)
        return jnp.where(lane < TAIL, y, 0.0)

    pm[...] = jnp.zeros(pm.shape, F32)
    pt[...] = jnp.zeros(pt.shape, F32)
    rest = [acc[j, 144:152, :] for j in range(NBLK)]
    for cz in range(2):
        mains = []
        tails = []
        for cy in range(2):
            c = 2 * cy + cz
            mains.append(rest[c][2:3] + rest[4 + c][3:4])
            tails.append(tail_lanes(rest[8], c)[2:3] + tail_lanes(rest[9], c)[3:4])
        pm[cz : cz + 1, :] = jnp.where(lev == 0, mains[0], mains[1])
        pt[cz : cz + 1, :] = jnp.where(lev == 0, tails[0], tails[1])
    add = upsampled(pm[0:16, :], pt[0:16, :])
    local2 = [rest[j] + add[j][0:8] for j in range(NBLK)]
    for c in range(8):
        cx, cy, cz = c >> 2, (c >> 1) & 1, c & 1
        tail = tail_lanes(local2[8 + cx], c)
        for p in range(2):
            r = 8 * cx + 4 * cy + 2 * p + cz
            pm[16 + r : 17 + r, :] = local2[c][p : p + 1]
            pt[16 + r : 17 + r, :] = tail[p : p + 1]
    add = upsampled(pm[16:32, :], pt[16:32, :])
    local1 = [acc[j, 128:144, :] + add[j] for j in range(NBLK)]
    for c in range(8):
        cx, cy, cz = c >> 2, (c >> 1) & 1, c & 1
        tail = tail_lanes(local1[8 + cx], c)
        for px in range(2):
            for py in range(2):
                r = 32 + 32 * (2 * px + cx) + 8 * (2 * py + cy) + cz
                q = 8 * px + 4 * py
                pm[pl.ds(r, 4, stride=2), :] = local1[c][q : q + 4]
                pt[pl.ds(r, 4, stride=2), :] = tail[q : q + 4]
    add = upsampled(pm[32:160, :], pt[32:160, :])
    stores = []
    for px in range(4):
        own = slice(32 * px, 32 * px + 32)
        for c in range(8):
            cx, cy, cz = c >> 2, (c >> 1) & 1, c & 1
            main = acc[c, own, :] + add[c][own]
            tail = tail_lanes(acc[8 + cx, own, :] + add[8 + cx][own], c)
            for py in range(4):
                q = 8 * py
                x, y = 2 * px + cx, 2 * py + cy
                om[8 * x + y, pl.ds(cz, 8, stride=2), :] = main[q : q + 8]
                ot[8 * x + y, pl.ds(cz, 8, stride=2), :] = tail[q : q + 8]
        for x in (2 * px, 2 * px + 1):
            for y in range(8):
                ob[x, y, :, 0:MAIN] = om[8 * x + y]
                ob[x, y, :, MAIN:CH] = ot[8 * x + y][:, 0:TAIL]
        pair = pl.ds(2 * px, 2)
        stores.append(pltpu.make_async_copy(ob.at[pair], out.at[pair], osem.at[px]))
        stores[-1].start()
    for c in stores:
        c.wait()


def shards(
    multipole_fine, multipole_mid, multipole_coarse, multipole_top, translation_ops, upsample_ops
):
    vmem = pltpu.VMEM
    far = pl.pallas_call(
        kernel,
        out_shape=pltpu.VMEM((NBLK, 160, MAIN), F32),
        in_specs=[pl.BlockSpec(memory_space=pltpu.HBM)] * 5,
        out_specs=pl.BlockSpec(memory_space=pltpu.VMEM),
        scratch_shapes=[
            vmem((7, 7, 7, ROWS, MAIN), BF),
            vmem((7, 7, 7, ROWS, TAIL), BF),
            vmem((12, 12, 16, CH), BF),
            vmem((8, 8, 8, CH), BF),
            vmem((6, 6, 4, CH), BF),
            vmem((7, 2, 2, CH), BF),
            vmem((12, 12, 32, MAIN), F32),
            vmem((12, 6, 32, MAIN), F32),
            vmem((8, 2, 48, MAIN), F32),
            vmem((8, 48, MAIN), F32),
            vmem((7, 6, 32, MAIN), F32),
            vmem((7, 3, 32, MAIN), F32),
            vmem((7, 6, 32, MAIN), F32),
            vmem((7, 3, 32, MAIN), F32),
            vmem((9, NBLK, 4, 32, MAIN), BF),
            vmem((9, NBLK, 32, MAIN), BF),
            vmem((9, NBLK, 32, MAIN), BF),
            vmem((9, NBLK, 32, MAIN), BF),
            vmem((9, NBLK, 32, MAIN), BF),
            vmem((9, NBLK, 32, MAIN), BF),
            vmem((7 * 36, ROWS, MAIN), BF),
            pltpu.SemaphoreType.DMA((32,)),
            pltpu.SemaphoreType.DMA((6,)),
            pltpu.SemaphoreType.DMA((11,)),
            pltpu.SemaphoreType.DMA((11,)),
        ],
        compiler_params=pltpu.CompilerParams(
            collective_id=0, has_side_effects=True, vmem_limit_bytes=56_000_000
        ),
        name="downward",
    )(multipole_fine, multipole_mid, multipole_coarse, multipole_top, translation_ops)
    return pl.pallas_call(
        finish,
        out_shape=jax.ShapeDtypeStruct((8, 8, 16, CH), F32),
        in_specs=[pl.BlockSpec(memory_space=pltpu.VMEM)] * 2,
        out_specs=pl.BlockSpec(memory_space=pl.ANY),
        scratch_shapes=[
            vmem((2, ROWS, MAIN), BF),
            vmem((160, MAIN), F32),
            vmem((160, MAIN), F32),
            vmem((64, 16, MAIN), F32),
            vmem((64, 16, MAIN), F32),
            vmem((8, 8, 16, CH), F32),
            pltpu.SemaphoreType.DMA((4,)),
        ],
        compiler_params=pltpu.CompilerParams(vmem_limit_bytes=24_000_000),
        name="upsample",
    )(far, upsample_ops)


def solution(mesh):
    placed = (
        P("space", None, None, None),
        P("space", None, None, None),
        P("space", None, None, None),
        P("space", None, None, None),
        P(),
        P(),
    )
    return jax.shard_map(
        shards,
        mesh=mesh,
        in_specs=placed,
        out_specs=P("space", "level", None, None),
        check_vma=False,
    )
```

```python
import jax
import jax.numpy as jnp
from jax import lax
from jax.experimental import pallas as pl
from jax.experimental.pallas import tpu as pltpu
from jax.sharding import PartitionSpec as P

BF = jnp.bfloat16
F32 = jnp.float32
MESH = pl.DeviceIdType.MESH
CH = 152
MAIN = 128
TAIL = CH - MAIN
ROWS = 160
NBLK = 10


def pad_tail(x):
    zeros = jnp.zeros(x.shape[:-1] + (MAIN - TAIL,), x.dtype)
    return jnp.concatenate([x, zeros], axis=x.ndim - 1)


def kernel(
    mf, mm, mc, mt, tr, acc,
    tm, tt, gb0, gb1, gb2, gb3,
    f0, t0, f1, t1, f2, t2, f3, t3,
    xm, xl, xr, xsm, xsl, xsr, v,
    tsem, gsem, send, recv,
):
    col = lax.axis_index("space")
    lev = lax.axis_index("level")
    n_col = lax.axis_size("space")
    par = col // 2
    base = 2 * par
    odd = lax.rem(col, 2)
    lo_ok = par > 0
    hi_ok = par < n_col // 2 - 1

    barrier = pltpu.get_barrier_semaphore()

    def greet(dev):
        pl.semaphore_signal(barrier, inc=1, device_id=(dev, lev), device_id_type=MESH)

    greet(base + 1 - odd)

    @pl.when(lo_ok)
    def _():
        greet(base - 2)
        greet(base - 1)

    @pl.when(hi_ok)
    def _():
        greet(base + 2)
        greet(base + 3)

    y0 = 6 * lev
    d0 = 2 * (1 - lev)
    y1 = 2 * lev
    loc0 = pltpu.make_async_copy(mf.at[:, pl.ds(y0, 10)], gb0.at[2:10, pl.ds(d0, 10)], gsem.at[0])
    loc1 = pltpu.make_async_copy(mm.at[:, pl.ds(y1, 6)], gb1.at[2:6, pl.ds(d0, 6)], gsem.at[1])
    loc2 = pltpu.make_async_copy(mc, gb2.at[2:4, pl.ds(d0, 4)], gsem.at[2])
    loc3 = pltpu.make_async_copy(mt, gb3.at[3:4], gsem.at[3])
    loc0.start()
    loc1.start()
    loc2.start()
    loc3.start()

    tcopies = {}

    def tcopy(kx, ysl, zsl, i):
        a = pltpu.make_async_copy(
            tr.at[kx, ysl, zsl, :, 0:MAIN], tm.at[kx, ysl, zsl, 0:CH, :], tsem.at[2 * i]
        )
        b = pltpu.make_async_copy(
            tr.at[kx, ysl, zsl, :, MAIN:CH], tt.at[kx, ysl, zsl, 0:CH, :], tsem.at[2 * i + 1]
        )
        a.start()
        b.start()
        tcopies.setdefault(kx, []).extend([a, b])

    idx = 0
    for kx in (3, 2, 4, 1, 0, 5, 6):
        if 2 <= kx <= 4:
            pieces = [
                (slice(0, 2), slice(0, 7)),
                (slice(5, 7), slice(0, 7)),
                (slice(2, 5), slice(0, 2)),
                (slice(2, 5), slice(5, 7)),
            ]
        else:
            pieces = [(slice(0, 7), slice(0, 7))]
        for ysl, zsl in pieces:
            tcopy(kx, ysl, zsl, idx)
            idx += 1
    def halo(src, dst, i, dev, j=None):
        return pltpu.make_async_remote_copy(
            src_ref=src, dst_ref=dst, send_sem=send.at[i], recv_sem=recv.at[i if j is None else j],
            device_id=(dev, lev), device_id_type=MESH,
        )

    rights = [
        halo(mf.at[6:8, pl.ds(y0, 10)], gb0.at[0:2, pl.ds(d0, 10)], 0, col + 1),
        halo(mm.at[2:4, pl.ds(y1, 6)], gb1.at[0:2, pl.ds(d0, 6)], 1, col + 1),
        halo(mc, gb2.at[0:2, pl.ds(d0, 4)], 2, col + 1),
    ]
    lefts = [
        halo(mf.at[0:2, pl.ds(y0, 10)], gb0.at[10:12, pl.ds(d0, 10)], 3, col - 1),
        halo(mm.at[0:2, pl.ds(y1, 6)], gb1.at[6:8, pl.ds(d0, 6)], 4, col - 1),
        halo(mc, gb2.at[4:6, pl.ds(d0, 4)], 5, col - 1),
    ]
    top_partner = halo(mt, gb3.at[pl.ds(2 + 2 * odd, 1)], 6, base + 1 - odd)
    top_low = [
        halo(mt, gb3.at[pl.ds(5 + odd - i, 1)], 7 + i, base - 2 + i, 7 + odd) for i in range(2)
    ]
    top_high = [
        halo(mt, gb3.at[pl.ds(1 + odd - i, 1)], 9 + i, base + 2 + i, 9 + odd) for i in range(2)
    ]
    n_greet = 1 + jnp.where(lo_ok, 2, 0) + jnp.where(hi_ok, 2, 0)
    z8 = jnp.zeros((8, MAIN), F32)
    gb0[:, pl.ds(10 * lev, 2)] = jnp.zeros((12, 2, 16, CH), BF)
    gb1[:, pl.ds(6 * lev, 2)] = jnp.zeros((8, 2, 8, CH), BF)
    gb2[:, pl.ds(4 * lev, 2)] = jnp.zeros((6, 2, 4, CH), BF)

    @pl.when(col == 0)
    def _():
        gb0[0:2] = jnp.zeros((2, 12, 16, CH), BF)
        gb1[0:2] = jnp.zeros((2, 8, 8, CH), BF)
        gb2[0:2] = jnp.zeros((2, 6, 4, CH), BF)

    @pl.when(col == n_col - 1)
    def _():
        gb0[10:12] = jnp.zeros((2, 12, 16, CH), BF)
        gb1[6:8] = jnp.zeros((2, 8, 8, CH), BF)
        gb2[4:6] = jnp.zeros((2, 6, 4, CH), BF)

    top0 = jnp.zeros((1, 2, 2, CH), BF)
    gb3[pl.ds(6 * odd, 1)] = top0

    @pl.when(par == 0)
    def _():
        gb3[0:1] = top0
        gb3[1:2] = top0
        gb3[pl.ds(2 * (1 - odd), 1)] = top0

    @pl.when(par == n_col // 2 - 1)
    def _():
        gb3[5:6] = top0
        gb3[6:7] = top0
        gb3[pl.ds(5 - odd, 1)] = top0

    def zero_edges(kx, _):
        for ky in range(7):
            tm[kx, ky, :, CH:ROWS, :] = jnp.zeros((7, ROWS - CH, MAIN), BF)
            tt[kx, ky, :, CH:ROWS, :] = jnp.zeros((7, ROWS - CH, TAIL), BF)
        return 0

    lax.fori_loop(0, 7, zero_edges, 0)

    def zero_pads(x, _):
        for y in range(12):
            f0[x, y, 0:8, :] = z8
            f0[x, y, 24:32, :] = z8
        for yp in range(6):
            t0[x, yp, 0:8, :] = z8
            t0[x, yp, 24:32, :] = z8
        return 0

    lax.fori_loop(0, 12, zero_pads, 0)

    def zero_coarse(x, _):
        f2[x] = jnp.zeros((6, 32, MAIN), F32)
        f3[x] = jnp.zeros((6, 32, MAIN), F32)
        t2[x] = jnp.zeros((3, 32, MAIN), F32)
        t3[x] = jnp.zeros((3, 32, MAIN), F32)
        return 0

    lax.fori_loop(0, 7, zero_coarse, 0)

    def zero_mid(x, _):
        for sy in range(2):
            f1[x, sy, 0:8, :] = z8
            f1[x, sy, 40:48, :] = z8
        t1[x, 0:8, :] = z8
        t1[x, 40:48, :] = z8
        return 0

    lax.fori_loop(0, 8, zero_mid, 0)

    def z_slots(tail, sy):
        even = lax.rem(lax.broadcasted_iota(jnp.int32, tail.shape, 0), 2) == 0
        a = pltpu.roll(tail, 64 * sy, 1) if sy else tail
        b = pltpu.roll(tail, 64 * sy + 32, 1)
        return jnp.where(even, a, b)

    def conv0(x):
        for yp in range(6):
            tails = []
            for sy in range(2):
                y = 2 * yp + sy
                f0[x, y, 8:24, :] = gb0[x, y, :, 0:MAIN].astype(F32)
                tails.append(z_slots(pad_tail(gb0[x, y, :, MAIN:CH].astype(F32)), sy))
            t0[x, yp, 8:24, :] = tails[0] + tails[1]

    def build0(xp, w, store):
        sty, stz = (w // 3, w % 3) if isinstance(w, int) else (w // 3, lax.rem(w, 3))
        for sx in range(2):
            x = 2 * xp + sx
            for sy in range(2):
                for sz in range(2):
                    rows = [
                        f0[x, 2 * (py + sty) + sy, pl.ds(6 + 2 * stz + sz, 8, stride=2), :]
                        for py in range(4)
                    ]
                    store(w, 4 * sx + 2 * sy + sz, jnp.concatenate(rows, axis=0).astype(BF))
            rows = [
                t0[x, py + sty, pl.ds(6 + 2 * stz, 8, stride=2), :]
                + t0[x, py + sty, pl.ds(7 + 2 * stz, 8, stride=2), :]
                for py in range(4)
            ]
            store(w, 8 + sx, jnp.concatenate(rows, axis=0).astype(BF))

    with jax.named_scope("conv_own"):
        loc0.wait()

        def own_conv(x, _):
            conv0(x)
            return 0

        lax.fori_loop(2, 10, own_conv, 0)

    with jax.named_scope("build_own"):

        def own_build(w, _):
            for xp in range(1, 5):

                def store(w, j, val, xp=xp):
                    xm[w, j, xp - 1] = val

                build0(xp, w, store)
            return 0

        lax.fori_loop(0, 9, own_build, 0)

    def conv1(x):
        for yp in range(4):
            tails = []
            for sy in range(2):
                y = 2 * yp + sy
                f1[x, sy, 8 + 8 * yp : 16 + 8 * yp, :] = gb1[x, y, :, 0:MAIN].astype(F32)
                tails.append(z_slots(pad_tail(gb1[x, y, :, MAIN:CH].astype(F32)), sy))
            t1[x, 8 + 8 * yp : 16 + 8 * yp, :] = tails[0] + tails[1]

    def conv2(x):
        for yp in range(3):
            tails = []
            for sy in range(2):
                y = 2 * yp + sy
                f2[x, y, 8:12, :] = gb2[x, y, :, 0:MAIN].astype(F32)
                tails.append(z_slots(pad_tail(gb2[x, y, :, MAIN:CH].astype(F32)), sy))
            t2[x, yp, 8:12, :] = tails[0] + tails[1]

    def conv3(x):
        tails = []
        for y in range(2):
            f3[x, 2 + y, 8:10, :] = gb3[x, y, :, 0:MAIN].astype(F32)
            tails.append(z_slots(pad_tail(gb3[x, y, :, MAIN:CH].astype(F32)), y))
        t3[x, 1, 8:10, :] = tails[0] + tails[1]

    def build_small(stx, sty, stz, store):
        row = lax.broadcasted_iota(jnp.int32, (8, MAIN), 0)
        pz = lax.rem(row, 4) + stz - 1
        inside = (pz >= 0) & (pz < 4)

        def put(j, one, two, three, four):
            one = [jnp.where(inside, p, 0.0) for p in one]
            rest = jnp.where(row < 2, two, 0.0)
            if three is not None:
                rest = jnp.where(row == 2, three, rest)
            if four is not None:
                rest = jnp.where(row == 3, four, rest)
            store(3 * sty + stz, j, jnp.concatenate(one + [rest, z8], axis=0).astype(BF))

        for sx in range(2):
            if isinstance(stx, int):
                three_x, four_x = ((3, None)[sx], None)
                keep = None
            else:
                three_x = 1 if sx == 0 else 2 + 2 * stx
                four_x = 2 * stx if sx == 0 else 5
                keep = (stx == 0) if sx == 0 else (stx == 2)

            def only(val, wanted):
                return val if keep is None or not wanted else jnp.where(keep, val, 0.0)

            def top(x, y, start, wanted):
                if x is None:
                    return None
                return only(f3[x, y, pl.ds(start + 2 * stz, 8, stride=2), :], wanted)

            def top_tail(x, start, wanted):
                if x is None:
                    return None
                return only(
                    t3[x, sty, pl.ds(start + 2 * stz, 8, stride=2), :]
                    + t3[x, sty, pl.ds(start + 1 + 2 * stz, 8, stride=2), :],
                    wanted,
                )

            for sy in range(2):
                for sz in range(2):
                    one = [
                        f1[2 * (px + stx) + sx, sy, pl.ds(6 + 8 * sty + 2 * stz + sz, 8, stride=2), :]
                        for px in range(2)
                    ]
                    y = 2 * sty + sy
                    two = f2[2 * stx + sx, y, pl.ds(6 + 2 * stz + sz, 8, stride=2), :]
                    three = top(three_x, y, 2 + sz, sx == 0)
                    four = top(four_x, y, sz, sx == 1)
                    put(4 * sx + 2 * sy + sz, one, two, three, four)
            one = [
                t1[2 * (px + stx) + sx, pl.ds(6 + 8 * sty + 2 * stz, 8, stride=2), :]
                + t1[2 * (px + stx) + sx, pl.ds(7 + 8 * sty + 2 * stz, 8, stride=2), :]
                for px in range(2)
            ]
            two = (
                t2[2 * stx + sx, sty, pl.ds(6 + 2 * stz, 8, stride=2), :]
                + t2[2 * stx + sx, sty, pl.ds(7 + 2 * stz, 8, stride=2), :]
            )
            put(8 + sx, one, two, top_tail(three_x, 2, sx == 0), top_tail(four_x, 0, sx == 1))

    def tail_unit(kx, rz):
        last = None
        for ky in range(7):
            a = pad_tail(tt[kx, ky, rz + 1])
            b = pad_tail(tt[kx, ky, rz])
            pair = a + pltpu.roll(b, 32, 1)
            if last is not None:
                v[(kx * 6 + ky - 1) * 6 + rz] = pair + last
            last = pltpu.roll(pair, 64, 1)

    def wait_t(*slabs):
        for kx in slabs:
            for c in tcopies[kx]:
                c.wait()

    with jax.named_scope("greet"):
        pl.semaphore_wait(barrier, n_greet)

        top_partner.start()

        @pl.when(lo_ok)
        def _():
            for c in top_low:
                c.start()

        @pl.when(hi_ok)
        def _():
            for c in top_high:
                c.start()

        @pl.when((col < n_col - 1) & (lev == 0))
        def _():
            for c in rights[::-1]:
                c.start()

        @pl.when((col > 0) & (lev == 1))
        def _():
            for c in lefts[::-1]:
                c.start()

    def zero_near(i, _):
        for kz in range(2, 5):
            tm[2 + i // 3, 2 + lax.rem(i, 3), kz, 0:CH, :] = jnp.zeros((CH, MAIN), BF)
            tt[2 + i // 3, 2 + lax.rem(i, 3), kz, 0:CH, :] = jnp.zeros((CH, TAIL), BF)
        return 0

    lax.fori_loop(0, 9, zero_near, 0)
    with jax.named_scope("conv_small"):
        loc1.wait()
        loc2.wait()
        loc3.wait()
        for x in range(2, 6):
            conv1(x)
        for x in range(2, 4):
            conv2(x)
        conv3(3)

    with jax.named_scope("build_small"):

        def small_mid(sty, _):
            def store(w, j, val):
                xsm[w, j] = val

            for stz in range(3):
                build_small(1, sty, stz, store)
            return 0

        lax.fori_loop(0, 3, small_mid, 0)

    with jax.named_scope("wait_t"):
        wait_t(3)

    def front(rz, _):
        tail_unit(3, rz)
        return 0

    def lhs_part(stx, w, j):
        if isinstance(stx, tuple):
            k, side = stx
            mid = xm[w, j, pl.ds(side, 3)].reshape(96, MAIN)
            rows = [(xl, xr)[k][w, j], mid, (xsl, xsr)[k][w, j]]
        else:
            rows = [xm[w, j].reshape(128, MAIN), xsm[w, j]]
        return jnp.concatenate(rows, axis=0)

    def near(step, s, c):
        return all(
            abs(2 * t - 2 + ((s >> b) & 1) - ((c >> b) & 1)) <= 1 for t, b in zip(step, (2, 1, 0))
        )

    def dot_n(cs, stx, sty, stzs, order=(0, 1, 2, 3, 4, 5, 6, 7)):
        two_sided = isinstance(stx, tuple)
        step_x = 2 * stx[1] if two_sided else stx
        parts = []
        blocks = []
        for stz in stzs:
            w = 3 * sty + stz
            rows = []
            lasts = []
            for s in order:
                sx, sy, sz = s >> 2, (s >> 1) & 1, s & 1
                pair = []
                for c in cs:
                    if c < 8:
                        kx = 2 * step_x + sx - (c >> 2) + 1
                        ky = 2 * sty + sy - ((c >> 1) & 1) + 1
                        kz = 2 * stz + sz - (c & 1) + 1
                        pair.append((tm[kx, ky, kz, 0:MAIN, :], tm[kx, ky, kz, MAIN:ROWS, :]))
                    else:
                        k = ((2 * step_x + sx - (c - 8) + 1) * 6 + 2 * sty + sy) * 6 + 2 * stz + sz
                        pair.append((v[k, 0:MAIN, :], v[k, MAIN:ROWS, :]))
                rows.append(jnp.concatenate([p[0] for p in pair], axis=1))
                lasts.append(jnp.concatenate([p[1] for p in pair], axis=1))
            for a in range(0, 8, 2):
                fixed = isinstance(sty, int) and not two_sided and cs[0] < 8
                if fixed and all(
                    near((stx, sty, stz), s, c) for s in order[a : a + 2] for c in cs
                ):
                    continue
                parts += [lhs_part(stx, w, order[a]), lhs_part(stx, w, order[a + 1])]
                blocks += rows[a : a + 2]
            parts += [lhs_part(stx, w, 8), lhs_part(stx, w, 9)]
            blocks += [lasts[order.index(s)] for s in range(8)]
        lhs = jnp.concatenate(parts, axis=1)
        rhs = jnp.concatenate(blocks, axis=0)
        res = jnp.dot(lhs, rhs, preferred_element_type=F32)
        for h, c in enumerate(cs):
            own = res[:, MAIN * h : MAIN * (h + 1)]
            if two_sided:
                side = stx[1]
                acc[c, pl.ds(pl.multiple_of(96 * side, 32), 32)] += own[0:32]
                acc[c, pl.ds(pl.multiple_of(32 - 32 * side, 32), 96)] += own[32:128]
                acc[c, 128:160] += own[128:160]
            else:
                acc[c] += own

    def block(stx, sty, stzs, fill):
        centre = stx == 1 and isinstance(sty, int) and sty == 1
        for n in range(4):
            if centre:
                first = 4 * (n >> 1) + (n & 1)
                dot_n((first, first + 2), stx, sty, stzs, (0, 2, 4, 6, 1, 3, 5, 7))
            else:
                dot_n((2 * n, 2 * n + 1), stx, sty, stzs)
            for k in range(n * len(fill) // 4, (n + 1) * len(fill) // 4):
                fill[k]()

    with jax.named_scope("front"):
        lax.fori_loop(0, 6, front, 0)
    acc[...] = jnp.zeros(acc.shape, F32)
    with jax.named_scope("wait_t"):
        wait_t(2, 4)
    with jax.named_scope("mxu1"):

        for i in range(2):
            units = [lambda q=q: tail_unit(2, 3 * i + q) for q in range(3)]
            units.append(lambda: tail_unit(4, i))

            @pl.when(lev >= 0)
            def _():
                block(1, 2 * i, (0, 1, 2), units)

    @pl.when((col < n_col - 1) & (lev == 1))
    def _():
        for c in rights[::-1]:
            c.start()

    @pl.when((col > 0) & (lev == 0))
    def _():
        for c in lefts[::-1]:
            c.start()

    with jax.named_scope("mxu1c"):
        block(1, 1, (0, 2), [lambda q=q: tail_unit(4, q) for q in range(2, 6)])

    def tail_dots(stx):
        def body(sty, _):
            dot_n((8, 9), stx, sty, (0, 1, 2))
            return 0

        with jax.named_scope("mxu_tail"):
            lax.fori_loop(0, 3, body, 0)

    tail_dots(1)

    with jax.named_scope("wait_halo"):

        halo(mt, gb3.at[pl.ds(4 - 2 * odd, 1)], 6, base + 1 - odd).wait_recv()

        @pl.when(lo_ok)
        def _():
            for i in range(2):
                halo(mt, gb3.at[pl.ds(1 + i - odd, 1)], 9 + i, base - 2 + i).wait_recv()

        @pl.when(hi_ok)
        def _():
            for i in range(2):
                halo(mt, gb3.at[pl.ds(5 + i - odd, 1)], 7 + i, base + 2 + i).wait_recv()

        @pl.when((col > 0) & (lev == 0))
        def _():
            for c in rights:
                c.wait_recv()

        @pl.when((col < n_col - 1) & (lev == 1))
        def _():
            for c in lefts:
                c.wait_recv()

    one_side = lev
    two_side = 1 - lev

    def convert(side):
        for x in range(2):
            conv0(10 * side + x)
            conv1(6 * side + x)
            conv2(4 * side + x)
        for x in range(3):
            conv3(4 * side + x)

    def edge(w, side, k):
        def store(w, j, val):
            (xl, xr)[k][w, j] = val

        def store_small(w, j, val):
            (xsl, xsr)[k][w, j] = val

        build0(5 * side, w, store)
        build_small(2 * side, w // 3, lax.rem(w, 3), store_small)

    with jax.named_scope("edges"):
        convert(one_side)

        def first_edge(sty, _):
            for q in range(3):
                edge(3 * sty + q, one_side, 0)
            return 0

        lax.fori_loop(0, 3, first_edge, 0)
    with jax.named_scope("wait_t"):
        wait_t(1, 0, 5, 6)

    def units_of(sty, slabs):
        return [lambda kx=kx, q=q: tail_unit(kx, 2 * sty + q) for q in range(2) for kx in slabs]

    def side_body(k, side, more):
        def body(sty, _):
            fill = units_of(sty, (1, 0) if k == 0 else (5, 6))
            for q in range(more):
                fill.append(lambda q=q: edge(more * sty - more + q, two_side, 1))
            block((k, side), sty, (0, 1, 2), fill)
            return 0

        return body

    with jax.named_scope("mxu02"):
        lax.fori_loop(0, 1, side_body(0, one_side, 0), 0)
    with jax.named_scope("wait_halo"):

        @pl.when((col > 0) & (lev == 1))
        def _():
            for c in rights:
                c.wait_recv()

        @pl.when((col < n_col - 1) & (lev == 0))
        def _():
            for c in lefts:
                c.wait_recv()

    with jax.named_scope("edges"):
        convert(two_side)
    with jax.named_scope("mxu02"):
        lax.fori_loop(1, 3, side_body(0, one_side, 4), 0)
    edge(jnp.int32(8), two_side, 1)
    with jax.named_scope("mxu02"):
        lax.fori_loop(0, 3, side_body(1, two_side, 0), 0)

    tail_dots((0, one_side))
    tail_dots((1, two_side))

    top_partner.wait_send()

    @pl.when(lo_ok)
    def _():
        for c in top_low:
            c.wait_send()

    @pl.when(hi_ok)
    def _():
        for c in top_high:
            c.wait_send()

    @pl.when(col < n_col - 1)
    def _():
        for c in rights:
            c.wait_send()

    @pl.when(col > 0)
    def _():
        for c in lefts:
            c.wait_send()


def finish(acc, up, out, vu, pm, pt, om, ot, ob, osem):
    lev = lax.axis_index("level")
    def up_rows(c, lo, hi, lane):
        return up[c >> 2, (c >> 1) & 1, c & 1, lo:hi, lane]

    for h in range(2):
        parts = [pad_tail(up[h, q >> 1, q & 1, :, MAIN:CH]) for q in range(4)]
        total = parts[0]
        for q in range(1, 4):
            total = total + pltpu.roll(parts[q], 32 * q, 1)
        vu[h, 0:CH, :] = total
        vu[h, CH:ROWS, :] = jnp.zeros((ROWS - CH, MAIN), BF)

    def upsampled(main, tail):
        rows = main.shape[0]
        hi_m = main.astype(BF)
        lo_m = (main - hi_m.astype(F32)).astype(BF)
        hi_t = tail.astype(BF).astype(F32)
        both = (hi_t + pltpu.roll(tail - hi_t, 32, 1)).astype(BF)
        lhs = jnp.concatenate([hi_m, lo_m, both], axis=1)

        def rhs_of(main, last):
            last = jnp.concatenate([last, jnp.zeros((ROWS - CH, MAIN), BF)], axis=0)
            return jnp.concatenate([main, main, last, last, jnp.zeros((64, MAIN), BF)], axis=0)

        cols = []
        for n in range(5):
            if n < 4:
                pair = [
                    rhs_of(up_rows(c, 0, MAIN, slice(0, MAIN)), up_rows(c, MAIN, CH, slice(0, MAIN)))
                    for c in (2 * n, 2 * n + 1)
                ]
            else:
                pair = [rhs_of(vu[h, 0:MAIN, :], vu[h, MAIN:CH, :]) for h in range(2)]
            res = jnp.dot(lhs, jnp.concatenate(pair, axis=1), preferred_element_type=F32)
            cols += [res[:, 0:MAIN], res[:, MAIN:]]
        return cols

    def tail_lanes(x, c):
        q = c & 3
        y = pltpu.roll(x, MAIN - 32 * q, 1) if q else x
        lane = lax.broadcasted_iota(jnp.int32, x.shape, 1)
        return jnp.where(lane < TAIL, y, 0.0)

    pm[...] = jnp.zeros(pm.shape, F32)
    pt[...] = jnp.zeros(pt.shape, F32)
    rest = [acc[j, 144:152, :] for j in range(NBLK)]
    for cz in range(2):
        mains = []
        tails = []
        for cy in range(2):
            c = 2 * cy + cz
            mains.append(rest[c][2:3] + rest[4 + c][3:4])
            tails.append(tail_lanes(rest[8], c)[2:3] + tail_lanes(rest[9], c)[3:4])
        pm[cz : cz + 1, :] = jnp.where(lev == 0, mains[0], mains[1])
        pt[cz : cz + 1, :] = jnp.where(lev == 0, tails[0], tails[1])
    add = upsampled(pm[0:16, :], pt[0:16, :])
    local2 = [rest[j] + add[j][0:8] for j in range(NBLK)]
    for c in range(8):
        cx, cy, cz = c >> 2, (c >> 1) & 1, c & 1
        tail = tail_lanes(local2[8 + cx], c)
        for p in range(2):
            r = 8 * cx + 4 * cy + 2 * p + cz
            pm[16 + r : 17 + r, :] = local2[c][p : p + 1]
            pt[16 + r : 17 + r, :] = tail[p : p + 1]
    add = upsampled(pm[16:32, :], pt[16:32, :])
    local1 = [acc[j, 128:144, :] + add[j] for j in range(NBLK)]
    for c in range(8):
        cx, cy, cz = c >> 2, (c >> 1) & 1, c & 1
        tail = tail_lanes(local1[8 + cx], c)
        for px in range(2):
            for py in range(2):
                r = 32 + 32 * (2 * px + cx) + 8 * (2 * py + cy) + cz
                q = 8 * px + 4 * py
                pm[pl.ds(r, 4, stride=2), :] = local1[c][q : q + 4]
                pt[pl.ds(r, 4, stride=2), :] = tail[q : q + 4]
    add = upsampled(pm[32:160, :], pt[32:160, :])
    stores = []
    for px in range(4):
        own = slice(32 * px, 32 * px + 32)
        for c in range(8):
            cx, cy, cz = c >> 2, (c >> 1) & 1, c & 1
            main = acc[c, own, :] + add[c][own]
            tail = tail_lanes(acc[8 + cx, own, :] + add[8 + cx][own], c)
            for py in range(4):
                q = 8 * py
                x, y = 2 * px + cx, 2 * py + cy
                om[8 * x + y, pl.ds(cz, 8, stride=2), :] = main[q : q + 8]
                ot[8 * x + y, pl.ds(cz, 8, stride=2), :] = tail[q : q + 8]
        for x in (2 * px, 2 * px + 1):
            for y in range(8):
                ob[x, y, :, 0:MAIN] = om[8 * x + y]
                ob[x, y, :, MAIN:CH] = ot[8 * x + y][:, 0:TAIL]
        pair = pl.ds(2 * px, 2)
        stores.append(pltpu.make_async_copy(ob.at[pair], out.at[pair], osem.at[px]))
        stores[-1].start()
    for c in stores:
        c.wait()


def shards(
    multipole_fine, multipole_mid, multipole_coarse, multipole_top, translation_ops, upsample_ops
):
    vmem = pltpu.VMEM
    far = pl.pallas_call(
        kernel,
        out_shape=pltpu.VMEM((NBLK, 160, MAIN), F32),
        in_specs=[pl.BlockSpec(memory_space=pltpu.HBM)] * 5,
        out_specs=pl.BlockSpec(memory_space=pltpu.VMEM),
        scratch_shapes=[
            vmem((7, 7, 7, ROWS, MAIN), BF),
            vmem((7, 7, 7, ROWS, TAIL), BF),
            vmem((12, 12, 16, CH), BF),
            vmem((8, 8, 8, CH), BF),
            vmem((6, 6, 4, CH), BF),
            vmem((7, 2, 2, CH), BF),
            vmem((12, 12, 32, MAIN), F32),
            vmem((12, 6, 32, MAIN), F32),
            vmem((8, 2, 48, MAIN), F32),
            vmem((8, 48, MAIN), F32),
            vmem((7, 6, 32, MAIN), F32),
            vmem((7, 3, 32, MAIN), F32),
            vmem((7, 6, 32, MAIN), F32),
            vmem((7, 3, 32, MAIN), F32),
            vmem((9, NBLK, 4, 32, MAIN), BF),
            vmem((9, NBLK, 32, MAIN), BF),
            vmem((9, NBLK, 32, MAIN), BF),
            vmem((9, NBLK, 32, MAIN), BF),
            vmem((9, NBLK, 32, MAIN), BF),
            vmem((9, NBLK, 32, MAIN), BF),
            vmem((7 * 36, ROWS, MAIN), BF),
            pltpu.SemaphoreType.DMA((32,)),
            pltpu.SemaphoreType.DMA((6,)),
            pltpu.SemaphoreType.DMA((11,)),
            pltpu.SemaphoreType.DMA((11,)),
        ],
        compiler_params=pltpu.CompilerParams(
            collective_id=0, has_side_effects=True, vmem_limit_bytes=56_000_000
        ),
        name="downward",
    )(multipole_fine, multipole_mid, multipole_coarse, multipole_top, translation_ops)
    return pl.pallas_call(
        finish,
        out_shape=jax.ShapeDtypeStruct((8, 8, 16, CH), F32),
        in_specs=[pl.BlockSpec(memory_space=pltpu.VMEM)] * 2,
        out_specs=pl.BlockSpec(memory_space=pl.ANY),
        scratch_shapes=[
            vmem((2, ROWS, MAIN), BF),
            vmem((160, MAIN), F32),
            vmem((160, MAIN), F32),
            vmem((64, 16, MAIN), F32),
            vmem((64, 16, MAIN), F32),
            vmem((8, 8, 16, CH), F32),
            pltpu.SemaphoreType.DMA((4,)),
        ],
        compiler_params=pltpu.CompilerParams(vmem_limit_bytes=24_000_000),
        name="upsample",
    )(far, upsample_ops)


def solution(mesh):
    placed = (
        P("space", None, None, None),
        P("space", None, None, None),
        P("space", None, None, None),
        P("space", None, None, None),
        P(),
        P(),
    )
    return jax.shard_map(
        shards,
        mesh=mesh,
        in_specs=placed,
        out_specs=P("space", "level", None, None),
        check_vma=False,
    )
```
